256 devices in a mesh: ens: 8 (over y, z_hi), lat: 8 (over z_lo, core), lon: 4 (over x).
Axes of the slice: x: 4, y: 4, z: 8 (z_hi: 2, z_lo: 4; z = z_hi * 4 + z_lo), core: 2. Of those that a mesh axis runs over, the one named last changes fastest.
Arguments:
- perturbation: float32 [8, 16, 128, 1024], P('ens', None, 'lat', 'lon'), may hold values from -6 to 6
- seed_ids: int32 [8], P('ens'), may hold values from 0 to 15
- amp_table: float32 [16, 16], replicated, may hold values from 0.5 to 2
- start_state: float32 [16, 128, 1024], P('ens', 'lat', 'lon'), may hold values from -2.5 to 2.5
- speeds: bfloat16 [4, 2, 16, 128, 1024], P(None, None, None, 'lat', 'lon'), may hold values from 0.039794922 to 0.29882812
- upwind: int32 [4, 16, 128, 1024], P(None, None, 'lat', 'lon'), may hold values from 0 to 3
- viscosity: float32 [16], replicated, may hold values from 0.02 to 0.08
- reaction: float32 [16], replicated, may hold values from 0.02 to 0.1
Outputs:
- final_perturbation: float32 [8, 16, 128, 1024], P('ens', None, 'lat', 'lon')
- final_state: float32 [16, 128, 1024], P('ens', 'lat', 'lon')
The draws below stay inside these ranges and needn't reach their ends.
Inputs may be any that keep to these rules, and one draw needn't show every extreme that they name: `upwind`: value mod 2 is 1 where the zonal wind blows eastward, floor of value / 2 is 1 where the meridional wind blows toward higher rows. `seed_ids`: A row index of amp_table.
All inputs are finite; a program needn't handle non-finite values.
Results may differ from the reference program's by a relative error of at most 0.0003.
Values sent between devices are 32-bit elements; how exact they have to be, the bound alone decides.
No kernel may reach another device: no remote copies, remote signals or barrier semaphores. Data moves between devices by JAX's collectives and lax.ppermute only.
A program may use at most 64 MiB of HBM per device.

```python
import math
import jax
import jax.numpy as jnp
from jax import lax

LEV = 16
STEPS = 4
BANK = 16
MEMBERS = 8
NLAT = 128
NLON = 1024


def touch_ends(values, stream_key, smallest, high):
    shape = values.shape
    spot = [jax.random.randint(jax.random.fold_in(stream_key, axis), (), 0, shape[axis]) for axis in range(len(shape))]
    values = values.at[tuple(spot)].set(smallest)
    longest = shape.index(max(shape))
    spot[longest] = (spot[longest] + 1) % shape[longest]
    return values.at[tuple(spot)].set(high)


def block_scale(key, extent, shards, smallest, top_value):
    level, own = 1.0, jax.random.fold_in(key, 6)
    for axis_at, parts in shards:
        draws = jnp.exp(jax.random.uniform(jax.random.fold_in(own, axis_at), (parts,), jnp.float32, smallest / len(shards), top_value / len(shards)))
        level = level * jnp.repeat(draws, extent[axis_at] // parts).reshape([-1 if axis == axis_at else 1 for axis in range(len(extent))])
    return level


def scatter_about(stream_key, extent, deviation, reach, cuts=(), dtype=jnp.bfloat16):
    level = block_scale(stream_key, extent, cuts, -0.22, 0.18) if cuts else 1.0
    values = jax.random.normal(stream_key, extent, jnp.float32) * deviation * level
    return jnp.minimum(jnp.maximum(values, -reach), reach).astype(dtype)


def setup_inputs(seed: int = 0) -> dict:
    keys = jax.random.split(jax.random.key(seed), 9)
    return {
        "perturbation": scatter_about(keys[0], (MEMBERS, LEV, NLAT, NLON), 1.0, 6.0, ((0, 8), (2, 8), (3, 4)), jnp.float32),
        "seed_ids": touch_ends(jax.random.randint(keys[1], (MEMBERS,), 0, BANK), jax.random.fold_in(keys[1], 1), 0, BANK - 1).astype(jnp.int32),
        "amp_table": jnp.clip(jnp.exp(jax.random.uniform(keys[2], (BANK, LEV), jnp.float32, math.log(0.5), math.log(2.0))), 0.5, 2.0),
        "start_state": scatter_about(keys[3], (LEV, NLAT, NLON), 0.7, 2.5, ((0, 8), (1, 8), (2, 4)), jnp.float32),
        "speeds": jnp.clip(jnp.exp(math.log(0.29882812) - 2.0161293 * jax.random.uniform(keys[4], (STEPS, 2, LEV, NLAT, NLON), jnp.float32) ** block_scale(keys[4], (STEPS, 2, LEV, NLAT, NLON), ((3, 8), (4, 4)), -0.2, 0.2)), 0.039794922, 0.29882812).astype(jnp.bfloat16),
        "upwind": touch_ends(jax.random.randint(keys[5], (STEPS, LEV, NLAT, NLON), 0, 4), jax.random.fold_in(keys[5], 1), 0, 3).astype(jnp.int32),
        "viscosity": jnp.clip(jnp.exp(jax.random.uniform(keys[6], (LEV,), jnp.float32, math.log(0.02), math.log(0.08))), 0.02, 0.08),
        "reaction": jnp.clip(jnp.exp(jax.random.uniform(keys[7], (LEV,), jnp.float32, math.log(0.02), math.log(0.1))), 0.02, 0.1),
    }


def stencil(current, below, above, western, eastern, speed_lon, speed_lat, direction, viscous):
    lon_side = jnp.where(direction % 2 == 1, western, eastern)
    lat_side = jnp.where(direction // 2 == 1, below, above)
    spread = western + eastern + below + above - 4.0 * current
    return current - speed_lon * (current - lon_side) - speed_lat * (current - lat_side) + viscous * spread


def apply_step(current, speeds, upwind, viscosity, step_index):
    widths = [(0, 0)] * (current.ndim - 2) + [(1, 1), (0, 0)]
    padded = jnp.pad(current, widths)
    below = padded[..., :-2, :]
    above = padded[..., 2:, :]
    western = jnp.roll(current, 1, axis=-1)
    eastern = jnp.roll(current, -1, axis=-1)
    speed_lon = speeds[step_index, 0].astype(jnp.float32)
    speed_lat = speeds[step_index, 1].astype(jnp.float32)
    return stencil(current, below, above, western, eastern, speed_lon, speed_lat, upwind[step_index], viscosity[:, None, None])


def reference(perturbation, seed_ids, amp_table, start_state, speeds, upwind, viscosity, reaction):
    rates = reaction[:, None, None]
    states = []
    current = start_state
    for step_index in range(STEPS):
        states.append(current)
        current = apply_step(current, speeds, upwind, viscosity, step_index) - rates * current * current * current

    def one_member(pair):
        member, table_row = pair
        delta = member * amp_table[table_row][:, None, None]
        for step_index in range(STEPS):
            past = states[step_index]
            delta = apply_step(delta, speeds, upwind, viscosity, step_index) - 3.0 * rates * past * past * delta
        return delta

    final = lax.map(one_member, (perturbation, seed_ids))
    return final, current
```

```python
import functools

import jax
import jax.numpy as jnp
from jax import lax
from jax.experimental import pallas as pl
from jax.experimental.pallas import tpu as pltpu
from jax.sharding import PartitionSpec as P

F32 = jnp.float32
I32 = jnp.int32
STEPS = 4
LEV = 16
COEF = 3
NCD = 1 + 3 * COEF
VMEM = pl.BlockSpec(memory_space=pltpu.VMEM)
SMEM = pl.BlockSpec(memory_space=pltpu.SMEM)


def lanes():
    return lax.broadcasted_iota(I32, (8, 128), 1)


def subs():
    return lax.broadcasted_iota(I32, (8, 128), 0)


def rows_at(r):
    return pl.ds(8 * r, 8)


def cols_at(c):
    return pl.ds(128 * c, 128)


def own_tiles(delta_ref, speeds_ref, upwind_ref, a, lev, c):
    if a == 0:
        return [delta_ref[0, lev, rows_at(r), cols_at(c)] for r in range(2)]
    step, kind = divmod(a - 1, 3)
    if kind < 2:
        both = speeds_ref[step, kind, lev, :, cols_at(c)].astype(F32)
        return [both[0:8], both[8:16]]
    return [upwind_ref[step, lev, rows_at(r), cols_at(c)].astype(F32) for r in range(2)]


def pack_columns(delta_ref, speeds_ref, upwind_ref, state_ref, out_ref):
    lane = lanes()
    for a in range(NCD):
        acc = [jnp.zeros((8, 128), F32)] * 2
        for lev in range(LEV):
            left = own_tiles(delta_ref, speeds_ref, upwind_ref, a, lev, 0)
            right = own_tiles(delta_ref, speeds_ref, upwind_ref, a, lev, 1)
            for r in range(2):
                edge = jnp.where(lane < 64, left[r], right[r])
                edge = pltpu.roll(edge, 8 * lev + 4 if 8 * lev + 4 < 128 else 8 * lev + 4 - 128, 1)
                acc[r] = jnp.where(lane // 8 == lev, edge, acc[r])
        for r in range(2):
            out_ref[a, rows_at(r), :] = acc[r]
    first = 2 * lax.axis_index("ens")
    acc = [jnp.zeros((8, 128), F32)] * 2
    for i in range(2):
        for r in range(2):
            edge = jnp.where(
                lane < 64, state_ref[i, rows_at(r), cols_at(0)], state_ref[i, rows_at(r), cols_at(1)]
            )
            edge = pltpu.roll(edge, 8 * (first + i) + 4, 1)
            acc[r] = jnp.where(lane // 8 == first + i, edge, acc[r])
    for r in range(2):
        out_ref[NCD, rows_at(r), :] = acc[r]


def strip_tile(own_ref, west_ref, east_ref, a, r, c):
    half = lanes() % 8 < 4
    own = own_ref[a, rows_at(r), :]
    if c == 0:
        return jnp.where(half, west_ref[a, rows_at(r), :], own)
    return jnp.where(half, own, east_ref[a, rows_at(r), :])


def state_block(state_ref, own_ref, west_ref, east_ref, out_ref):
    out_ref[0:2] = state_ref[...]
    for r in range(2):
        for c in range(2):
            out_ref[2, rows_at(r), cols_at(c)] = strip_tile(own_ref, west_ref, east_ref, NCD, r, c)


def join_pair(own_ref, other_ref, out_ref):
    half = lax.rem(lax.axis_index("ens"), 2)
    out_ref[pl.ds(2 * half, 2)] = own_ref[0:2]
    out_ref[pl.ds(2 - 2 * half, 2)] = other_ref[0:2]
    out_ref[4] = own_ref[2] + other_ref[2]


def merge_rows(pieces):
    sub = subs()
    acc = jnp.zeros((8, 128), F32)
    for tile, shift, first, last in pieces:
        if shift % 8:
            tile = pltpu.roll(tile, shift % 8, 0)
        acc = jnp.where((sub >= first) & (sub <= last), tile, acc)
    return acc


def pack_rows(delta_ref, speeds_ref, upwind_ref, own_ref, west_ref, east_ref, strip_ref, down_ref, up_ref):
    def put(lev, c, tiles):
        for kind in range(3):
            k0, k1, k2 = (tiles[1 + 3 * step + kind] for step in range(3))
            d = tiles[0]
            low = [(k0[0], 0, 0, 2), (k1[0], 3, 3, 4), (k2[0], 5, 5, 5)]
            high = [(k0[1], 0, 5, 7), (k1[1], -3, 3, 4), (k2[1], -5, 2, 2)]
            if kind == 0:
                low.append((d[0], 6, 6, 7))
                high.append((d[1], -4, 0, 1))
            if kind == 1:
                low.append((d[0], 4, 6, 7))
                high.append((d[1], -6, 0, 1))
            down_ref[lev, rows_at(kind), cols_at(c)] = merge_rows(low)
            up_ref[lev, rows_at(kind), cols_at(c)] = merge_rows(high)

    for c in range(2):
        tiles = []
        for a in range(NCD):
            pair = [strip_tile(own_ref, west_ref, east_ref, a, r, c) for r in range(2)]
            for r in range(2):
                strip_ref[a, rows_at(r), cols_at(c)] = pair[r]
            tiles.append(pair)
        put(LEV, c, tiles)

    def body(lev, carry):
        for c in range(2):
            put(lev, c, [own_tiles(delta_ref, speeds_ref, upwind_ref, a, lev, c) for a in range(NCD)])
        return carry

    lax.fori_loop(0, LEV, body, 0)


def full_state(b0_ref, b1_ref, b2_ref, b3_ref, out_ref, down_ref, up_ref):
    mine = lax.axis_index("ens") // 2
    blocks = (b0_ref, b1_ref, b2_ref, b3_ref)
    for ahead in range(4):
        out_ref[pl.ds(4 * lax.rem(mine + ahead, 4), 4)] = blocks[ahead][0:4]
    out_ref[LEV] = (b0_ref[4] + b1_ref[4]) + (b2_ref[4] + b3_ref[4])
    low = subs() < 4
    for p in range(9):
        for c in range(2):
            a0, a1 = out_ref[2 * p, rows_at(0), cols_at(c)], out_ref[2 * p, rows_at(1), cols_at(c)]
            if p < 8:
                b0 = pltpu.roll(out_ref[2 * p + 1, rows_at(0), cols_at(c)], 4, 0)
                b1 = pltpu.roll(out_ref[2 * p + 1, rows_at(1), cols_at(c)], 4, 0)
            else:
                b0, b1 = a0, a1
            down_ref[p, :, cols_at(c)] = jnp.where(low, a0, b0)
            up_ref[p, :, cols_at(c)] = jnp.where(low, b1, a1)


def advance(
    seed_ref, table_ref, visc_ref, rate_ref,
    delta_ref, speeds_ref, upwind_ref, strip_ref, north_ref, south_ref,
    state_ref, snorth_ref, ssouth_ref,
    delta_out, state_out,
    edge_state, edge_delta, finals,
):
    lane, sub = lanes(), subs()
    band = lax.axis_index("lat")
    first = 2 * lax.axis_index("ens")
    seed = seed_ref[0]
    inside = jnp.where(
        sub < 4,
        jnp.where(band < lax.axis_size("lat") - 1, 1.0, 0.0).astype(F32),
        jnp.where(band > 0, 1.0, 0.0).astype(F32),
    )
    keep = [(sub <= 2, sub >= 5), (sub <= 1, sub >= 6), (sub <= 0, sub >= 7)]

    def halo_coef(lev, kind, step, c):
        north = north_ref[lev, rows_at(kind), cols_at(c)]
        south = south_ref[lev, rows_at(kind), cols_at(c)]
        shift = (0, 3, 5)[step]
        if shift:
            north = pltpu.roll(north, 8 - shift, 0)
            south = pltpu.roll(south, shift, 0)
        low, high = keep[step]
        return jnp.where(low, north, jnp.where(high, south, 0.0))

    def halo_delta(lev, c):
        n0 = pltpu.roll(north_ref[lev, rows_at(0), cols_at(c)], 2, 0)
        n1 = pltpu.roll(north_ref[lev, rows_at(1), cols_at(c)], 4, 0)
        s0 = pltpu.roll(south_ref[lev, rows_at(0), cols_at(c)], 4, 0)
        s1 = pltpu.roll(south_ref[lev, rows_at(1), cols_at(c)], 6, 0)
        return jnp.where(sub < 2, n0, jnp.where(sub < 4, n1, jnp.where(sub < 6, s0, s1)))

    def halo_state(p, odd, c):
        north, south = snorth_ref[p, :, cols_at(c)], ssouth_ref[p, :, cols_at(c)]
        if odd:
            return pltpu.roll(jnp.where(sub < 4, south, north), 4, 0)
        return jnp.where(sub < 4, north, south)

    def sides(f, fix_west, fix_east):
        west, east = [], []
        for r, (left, right) in enumerate(f):
            wl, wr = pltpu.roll(left, 1, 1), pltpu.roll(right, 1, 1)
            el, er = pltpu.roll(left, 127, 1), pltpu.roll(right, 127, 1)
            if fix_west is None:
                west.append((wl, wr))
                east.append((el, er))
            else:
                west.append((jnp.where(lane == 0, fix_west[r], wl), jnp.where(lane == 0, wl, wr)))
                east.append((jnp.where(lane == 127, er, el), jnp.where(lane == 127, fix_east[r], er)))
        return west, east

    def ends(f):
        below, above = [], []
        down = [[pltpu.roll(f[r][c], 1, 0) for c in range(2)] for r in range(3)]
        up = [[pltpu.roll(f[r][c], 7, 0) for c in range(2)] for r in range(3)]
        for r in range(3):
            below.append([jnp.where(sub == 0, down[(r + 2) % 3][c], down[r][c]) for c in range(2)])
            above.append([jnp.where(sub == 7, up[(r + 1) % 3][c], up[r][c]) for c in range(2)])
        return below, above

    def run(state, delta, visc, rate, coefs, edges, before):
        for step in range(STEPS):
            before(step, state, delta)
            if step == STEPS - 1 and edges is None:
                return state, delta
            count = 3 if step < STEPS - 1 else 2
            fixes = [None] * 4 if edges is None else edges(step, count)
            ws, es = sides(state[:count], fixes[0], fixes[1])
            wd, ed = sides(delta[:count], fixes[2], fixes[3])
            ss, ns = ends(state)
            sd, nd = ends(delta)
            next_state, next_delta = [], []
            for r in range(count):
                row_s, row_d = [], []
                for c in range(2):
                    s, t, m = coefs(step, r, c)
                    v = visc[c] if r < 2 else visc[c] * inside
                    vs, vt = v + s, v + t
                    eastward, northward = (m & 1) == 1, m >= 2
                    cw, ce = jnp.where(eastward, vs, v), jnp.where(eastward, v, vs)
                    cs, cn = jnp.where(northward, vt, v), jnp.where(northward, v, vt)
                    c0 = ((1.0 - 2.0 * v) - vs) - vt
                    f, d = state[r][c], delta[r][c]
                    loss = rate[c] * (f * f)
                    row_s.append(
                        ((c0 - loss) * f + cw * ws[r][c]) + (ce * es[r][c] + cs * ss[r][c]) + cn * ns[r][c]
                    )
                    row_d.append(
                        ((c0 - 3.0 * loss) * d + cw * wd[r][c]) + (ce * ed[r][c] + cs * sd[r][c]) + cn * nd[r][c]
                    )
                next_state.append(row_s)
                next_delta.append(row_d)
            state, delta = next_state, next_delta
        return state, delta

    visc = rate = amp = jnp.zeros((8, 128), F32)
    for lev in range(LEV):
        here = lane // 8 == lev
        visc = jnp.where(here, visc_ref[lev], visc)
        rate = jnp.where(here, rate_ref[lev], rate)
        amp = jnp.where(here, table_ref[seed, lev], amp)

    def strip_coefs(step, r, c):
        out = []
        for kind in range(3):
            if r < 2:
                out.append(strip_ref[1 + 3 * step + kind, rows_at(r), cols_at(c)])
            else:
                out.append(halo_coef(LEV, kind, step, c))
        return out[0], out[1], out[2].astype(I32)

    def strip_before(step, state, delta):
        for r in range(3):
            for c in range(2):
                edge_state[step, c, rows_at(r), :] = state[r][c]
                edge_delta[step, c, rows_at(r), :] = delta[r][c]

    state = [[state_ref[LEV, rows_at(r), cols_at(c)] for c in range(2)] for r in range(2)]
    state.append([halo_state(8, False, c) for c in range(2)])
    delta = [[strip_ref[0, rows_at(r), cols_at(c)] * amp for c in range(2)] for r in range(2)]
    delta.append([halo_delta(LEV, c) * amp for c in range(2)])
    run(state, delta, [visc] * 2, [rate] * 2, strip_coefs, None, strip_before)

    def one_level(p, odd):
        lev = 2 * p + odd
        visc = [jnp.full((8, 128), visc_ref[lev], F32)] * 2
        rate = [jnp.full((8, 128), rate_ref[lev], F32)] * 2
        amp = table_ref[seed, lev]

        def coefs(step, r, c):
            if r < 2:
                s = speeds_ref[step, 0, lev, :, cols_at(c)].astype(F32)[8 * r : 8 * r + 8]
                t = speeds_ref[step, 1, lev, :, cols_at(c)].astype(F32)[8 * r : 8 * r + 8]
                return s, t, upwind_ref[step, lev, rows_at(r), cols_at(c)]
            s, t, m = (halo_coef(lev, kind, step, c) for kind in range(3))
            return s, t, m.astype(I32)

        def edges(step, count):
            to_first = lax.rem(253 - 8 * lev, 128)
            to_last = lax.rem(251 - 8 * lev, 128)
            out = []
            for ref in (edge_state, edge_delta):
                out.append([pltpu.roll(ref[step, 0, rows_at(r), :], to_first, 1) for r in range(count)])
                out.append([pltpu.roll(ref[step, 1, rows_at(r), :], to_last, 1) for r in range(count)])
            return out

        state = [[state_ref[lev, rows_at(r), cols_at(c)] for c in range(2)] for r in range(2)]
        state.append([halo_state(p, odd, c) for c in range(2)])
        delta = [[delta_ref[0, lev, rows_at(r), cols_at(c)] * amp for c in range(2)] for r in range(2)]
        delta.append([halo_delta(lev, c) * amp for c in range(2)])
        state, delta = run(state, delta, visc, rate, coefs, edges, lambda *unused: None)
        for r in range(2):
            for c in range(2):
                finals[lev, rows_at(r), cols_at(c)] = state[r][c]
                delta_out[0, lev, rows_at(r), cols_at(c)] = delta[r][c]

    def body(p, carry):
        one_level(p, 0)
        one_level(p, 1)
        return carry

    lax.fori_loop(0, LEV // 2, body, 0)
    state_out[...] = finals[pl.ds(first, 2)]


def call(kernel, name, shapes, specs, scratch=(), cost=None):
    out = [jax.ShapeDtypeStruct(shape, F32) for shape in shapes]
    single = len(out) == 1
    return pl.pallas_call(
        kernel,
        name=name,
        out_shape=out[0] if single else out,
        in_specs=specs,
        out_specs=VMEM if single else [VMEM] * len(out),
        scratch_shapes=scratch,
        cost_estimate=pl.CostEstimate(flops=cost or 100000, bytes_accessed=cost or 100000, transcendentals=0),
    )


def per_device(perturbation, seed_ids, amp_table, start_state, speeds, upwind, viscosity, reaction):
    n_lat, n_lon, n_ens = lax.axis_size("lat"), lax.axis_size("lon"), lax.axis_size("ens")
    north = [(i, i + 1) for i in range(n_lat - 1)]
    south = [(j, i) for i, j in north]
    eastward = [(i, (i + 1) % n_lon) for i in range(n_lon)]
    westward = [(j, i) for i, j in eastward]

    columns = call(pack_columns, "pack_columns", [(NCD + 1, 16, 128)], [VMEM] * 4)(
        perturbation, speeds, upwind, start_state
    )
    from_west = lax.ppermute(columns, "lon", eastward)
    from_east = lax.ppermute(columns, "lon", westward)
    block = call(state_block, "state_block", [(3, 16, 256)], [VMEM] * 4)(
        start_state, columns, from_west, from_east
    )
    other = lax.ppermute(block, "ens", [(i, i ^ 1) for i in range(n_ens)])
    strips, down, up = call(
        pack_rows, "pack_rows", [(NCD, 16, 256), (LEV + 1, 24, 256), (LEV + 1, 24, 256)], [VMEM] * 6
    )(perturbation, speeds, upwind, columns, from_west, from_east)
    cd_north = lax.ppermute(down, "lat", south)
    cd_south = lax.ppermute(up, "lat", north)
    quad = call(join_pair, "join_pair", [(5, 16, 256)], [VMEM] * 2)(block, other)
    ahead = [
        lax.ppermute(quad, "ens", [((i + 2 * j) % n_ens, i) for i in range(n_ens)]) for j in (1, 2, 3)
    ]
    states, state_down, state_up = call(
        full_state, "full_state", [(LEV + 1, 16, 256), (9, 8, 256), (9, 8, 256)], [VMEM] * 4
    )(quad, *ahead)
    st_north = lax.ppermute(state_down, "lat", south)
    st_south = lax.ppermute(state_up, "lat", north)
    edge = pltpu.VMEM((STEPS, 2, 24, 128), F32)
    return call(
        advance,
        "advance",
        [(1, LEV, 16, 256), (2, 16, 256)],
        [SMEM] * 4 + [VMEM] * 9,
        scratch=[edge, edge, pltpu.VMEM((LEV, 16, 256), F32)],
        cost=10000000,
    )(
        seed_ids, amp_table, viscosity, reaction,
        perturbation, speeds, upwind, strips, cd_north, cd_south,
        states, st_north, st_south,
    )


def solution(mesh):
    step = jax.shard_map(
        per_device,
        mesh=mesh,
        in_specs=(
            P("ens", None, "lat", "lon"),
            P("ens"),
            P(),
            P("ens", "lat", "lon"),
            P(None, None, None, "lat", "lon"),
            P(None, None, "lat", "lon"),
            P(),
            P(),
        ),
        out_specs=(P("ens", None, "lat", "lon"), P("ens", "lat", "lon")),
        check_vma=False,
    )
    return lambda *args: tuple(step(*args))
```

```python
import jax
import jax.numpy as jnp
from jax import lax
from jax.experimental import pallas as pl
from jax.experimental.pallas import tpu as pltpu
from jax.sharding import PartitionSpec as P


F32 = jnp.float32
I32 = jnp.int32
STEPS = 4
LEV = 16
COEF = 3
NCD = 1 + 3 * COEF
VMEM = pl.BlockSpec(memory_space=pltpu.VMEM)
SMEM = pl.BlockSpec(memory_space=pltpu.SMEM)


def lanes():
    return lax.broadcasted_iota(I32, (8, 128), 1)


def subs():
    return lax.broadcasted_iota(I32, (8, 128), 0)


def rows_at(r):
    return pl.ds(8 * r, 8)


def cols_at(c):
    return pl.ds(128 * c, 128)


def own_tiles(delta_ref, speeds_ref, upwind_ref, a, lev, c):
    if a == 0:
        return [delta_ref[0, lev, rows_at(r), cols_at(c)] for r in range(2)]
    step, kind = divmod(a - 1, 3)
    if kind < 2:
        both = speeds_ref[step, kind, lev, :, cols_at(c)].astype(F32)
        return [both[0:8], both[8:16]]
    return [upwind_ref[step, lev, rows_at(r), cols_at(c)].astype(F32) for r in range(2)]


def slot(acc, left, right, lev):
    lane = lanes()
    edge = pltpu.roll(jnp.where(lane < 64, left, right), 8 * lev + 4, 1)
    return jnp.where(lane // 8 == lev, edge, acc)


def pack_columns(delta_ref, speeds_ref, upwind_ref, out_ref):
    for a in range(NCD):
        acc = [jnp.zeros((8, 128), F32)] * 2
        for lev in range(LEV):
            left = own_tiles(delta_ref, speeds_ref, upwind_ref, a, lev, 0)
            right = own_tiles(delta_ref, speeds_ref, upwind_ref, a, lev, 1)
            acc = [slot(acc[r], left[r], right[r], lev) for r in range(2)]
        for r in range(2):
            out_ref[a, rows_at(r), :] = acc[r]


def strip_tile(own_ref, west_ref, east_ref, a, r, c):
    half = lanes() % 8 < 4
    own = own_ref[a, rows_at(r), :]
    if c == 0:
        return jnp.where(half, west_ref[a, rows_at(r), :], own)
    return jnp.where(half, own, east_ref[a, rows_at(r), :])


def join_pair(own_ref, other_ref, out_ref):
    half = lax.rem(lax.axis_index("ens"), 2)
    out_ref[pl.ds(2 * half, 2)] = own_ref[...]
    out_ref[pl.ds(2 - 2 * half, 2)] = other_ref[...]


def merge_rows(pieces):
    sub = subs()
    acc = jnp.zeros((8, 128), F32)
    for tile, shift, first, last in pieces:
        if shift % 8:
            tile = pltpu.roll(tile, shift % 8, 0)
        acc = jnp.where((sub >= first) & (sub <= last), tile, acc)
    return acc


def pack_rows(delta_ref, speeds_ref, upwind_ref, own_ref, west_ref, east_ref, strip_ref, down_ref, up_ref):
    def put(lev, c, tiles):
        for kind in range(3):
            k0, k1, k2 = (tiles[1 + 3 * step + kind] for step in range(3))
            d = tiles[0]
            low = [(k0[0], 0, 0, 2), (k1[0], 3, 3, 4), (k2[0], 5, 5, 5)]
            high = [(k0[1], 0, 5, 7), (k1[1], -3, 3, 4), (k2[1], -5, 2, 2)]
            if kind == 0:
                low.append((d[0], 6, 6, 7))
                high.append((d[1], -4, 0, 1))
            if kind == 1:
                low.append((d[0], 4, 6, 7))
                high.append((d[1], -6, 0, 1))
            down_ref[lev, rows_at(kind), cols_at(c)] = merge_rows(low)
            up_ref[lev, rows_at(kind), cols_at(c)] = merge_rows(high)

    for c in range(2):
        tiles = []
        for a in range(NCD):
            pair = [strip_tile(own_ref, west_ref, east_ref, a, r, c) for r in range(2)]
            for r in range(2):
                strip_ref[a, rows_at(r), cols_at(c)] = pair[r]
            tiles.append(pair)
        put(LEV, c, tiles)

    def body(lev, carry):
        for c in range(2):
            put(lev, c, [own_tiles(delta_ref, speeds_ref, upwind_ref, a, lev, c) for a in range(NCD)])
        return carry

    lax.fori_loop(0, LEV, body, 0)


def join_all(b0_ref, b1_ref, b2_ref, b3_ref, out_ref, columns_ref):
    mine = lax.axis_index("ens") // 2
    acc = [jnp.zeros((8, 128), F32)] * 2
    for ahead, ref in enumerate((b0_ref, b1_ref, b2_ref, b3_ref)):
        base = 4 * lax.rem(mine + ahead, 4)
        out_ref[pl.ds(base, 4)] = ref[...]
        for i in range(4):
            for r in range(2):
                left, right = (ref[i, rows_at(r), cols_at(c)] for c in range(2))
                acc[r] = slot(acc[r], left, right, base + i)
    for r in range(2):
        columns_ref[0, rows_at(r), :] = acc[r]


def state_rows(state_ref, own_ref, west_ref, east_ref, strip_ref, down_ref, up_ref):
    low = subs() < 4
    for c in range(2):
        pair = [strip_tile(own_ref, west_ref, east_ref, 0, r, c) for r in range(2)]
        for r in range(2):
            strip_ref[rows_at(r), cols_at(c)] = pair[r]
        down_ref[8, :, cols_at(c)] = pair[0]
        up_ref[8, :, cols_at(c)] = pair[1]
        for p in range(8):
            a0, a1 = (state_ref[2 * p, rows_at(r), cols_at(c)] for r in range(2))
            b0, b1 = (pltpu.roll(state_ref[2 * p + 1, rows_at(r), cols_at(c)], 4, 0) for r in range(2))
            down_ref[p, :, cols_at(c)] = jnp.where(low, a0, b0)
            up_ref[p, :, cols_at(c)] = jnp.where(low, b1, a1)


def advance(
    seed_ref, table_ref, visc_ref, rate_ref,
    delta_ref, speeds_ref, upwind_ref, strip_ref, north_ref, south_ref,
    state_ref, state_strip_ref, snorth_ref, ssouth_ref,
    delta_out, state_out,
    edge_state, edge_delta, finals,
):
    lane, sub = lanes(), subs()
    band = lax.axis_index("lat")
    first = 2 * lax.axis_index("ens")
    seed = seed_ref[0]
    inside = jnp.where(
        sub < 4,
        jnp.where(band < lax.axis_size("lat") - 1, 1.0, 0.0).astype(F32),
        jnp.where(band > 0, 1.0, 0.0).astype(F32),
    )
    keep = [(sub <= 2, sub >= 5), (sub <= 1, sub >= 6), (sub <= 0, sub >= 7)]

    def halo_coef(lev, kind, step, c):
        north = north_ref[lev, rows_at(kind), cols_at(c)]
        south = south_ref[lev, rows_at(kind), cols_at(c)]
        shift = (0, 3, 5)[step]
        if shift:
            north = pltpu.roll(north, 8 - shift, 0)
            south = pltpu.roll(south, shift, 0)
        low, high = keep[step]
        return jnp.where(low, north, jnp.where(high, south, 0.0))

    def halo_delta(lev, c):
        n0 = pltpu.roll(north_ref[lev, rows_at(0), cols_at(c)], 2, 0)
        n1 = pltpu.roll(north_ref[lev, rows_at(1), cols_at(c)], 4, 0)
        s0 = pltpu.roll(south_ref[lev, rows_at(0), cols_at(c)], 4, 0)
        s1 = pltpu.roll(south_ref[lev, rows_at(1), cols_at(c)], 6, 0)
        return jnp.where(sub < 2, n0, jnp.where(sub < 4, n1, jnp.where(sub < 6, s0, s1)))

    def halo_state(p, odd, c):
        north, south = snorth_ref[p, :, cols_at(c)], ssouth_ref[p, :, cols_at(c)]
        if odd:
            return pltpu.roll(jnp.where(sub < 4, south, north), 4, 0)
        return jnp.where(sub < 4, north, south)

    def sides(f, fix_west, fix_east):
        west, east = [], []
        for r, (left, right) in enumerate(f):
            wl, wr = pltpu.roll(left, 1, 1), pltpu.roll(right, 1, 1)
            el, er = pltpu.roll(left, 127, 1), pltpu.roll(right, 127, 1)
            if fix_west is None:
                west.append((wl, wr))
                east.append((el, er))
            else:
                west.append((jnp.where(lane == 0, fix_west[r], wl), jnp.where(lane == 0, wl, wr)))
                east.append((jnp.where(lane == 127, er, el), jnp.where(lane == 127, fix_east[r], er)))
        return west, east

    def ends(f):
        below, above = [], []
        down = [[pltpu.roll(f[r][c], 1, 0) for c in range(2)] for r in range(3)]
        up = [[pltpu.roll(f[r][c], 7, 0) for c in range(2)] for r in range(3)]
        for r in range(3):
            below.append([jnp.where(sub == 0, down[(r + 2) % 3][c], down[r][c]) for c in range(2)])
            above.append([jnp.where(sub == 7, up[(r + 1) % 3][c], up[r][c]) for c in range(2)])
        return below, above

    def run(state, delta, visc, rate, coefs, edges, before):
        for step in range(STEPS):
            before(step, state, delta)
            if step == STEPS - 1 and edges is None:
                return state, delta
            count = 3 if step < STEPS - 1 else 2
            fixes = [None] * 4 if edges is None else edges(step, count)
            ws, es = sides(state[:count], fixes[0], fixes[1])
            wd, ed = sides(delta[:count], fixes[2], fixes[3])
            ss, ns = ends(state)
            sd, nd = ends(delta)
            next_state, next_delta = [], []
            for r in range(count):
                row_s, row_d = [], []
                for c in range(2):
                    s, t, m = coefs(step, r, c)
                    v = visc[c] if r < 2 else visc[c] * inside
                    vs, vt = v + s, v + t
                    eastward, northward = (m & 1) == 1, m >= 2
                    cw, ce = jnp.where(eastward, vs, v), jnp.where(eastward, v, vs)
                    cs, cn = jnp.where(northward, vt, v), jnp.where(northward, v, vt)
                    c0 = ((1.0 - 2.0 * v) - vs) - vt
                    f, d = state[r][c], delta[r][c]
                    loss = rate[c] * (f * f)
                    row_s.append(
                        ((c0 - loss) * f + cw * ws[r][c]) + (ce * es[r][c] + cs * ss[r][c]) + cn * ns[r][c]
                    )
                    row_d.append(
                        ((c0 - 3.0 * loss) * d + cw * wd[r][c]) + (ce * ed[r][c] + cs * sd[r][c]) + cn * nd[r][c]
                    )
                next_state.append(row_s)
                next_delta.append(row_d)
            state, delta = next_state, next_delta
        return state, delta

    visc = rate = amp = jnp.zeros((8, 128), F32)
    for lev in range(LEV):
        here = lane // 8 == lev
        visc = jnp.where(here, visc_ref[lev], visc)
        rate = jnp.where(here, rate_ref[lev], rate)
        amp = jnp.where(here, table_ref[seed, lev], amp)

    def strip_coefs(step, r, c):
        out = []
        for kind in range(3):
            if r < 2:
                out.append(strip_ref[1 + 3 * step + kind, rows_at(r), cols_at(c)])
            else:
                out.append(halo_coef(LEV, kind, step, c))
        return out[0], out[1], out[2].astype(I32)

    def strip_before(step, state, delta):
        for r in range(3):
            for c in range(2):
                edge_state[step, c, rows_at(r), :] = state[r][c]
                edge_delta[step, c, rows_at(r), :] = delta[r][c]

    state = [[state_strip_ref[rows_at(r), cols_at(c)] for c in range(2)] for r in range(2)]
    state.append([halo_state(8, False, c) for c in range(2)])
    delta = [[strip_ref[0, rows_at(r), cols_at(c)] * amp for c in range(2)] for r in range(2)]
    delta.append([halo_delta(LEV, c) * amp for c in range(2)])
    run(state, delta, [visc] * 2, [rate] * 2, strip_coefs, None, strip_before)

    def one_level(p, odd):
        lev = 2 * p + odd
        visc = [jnp.full((8, 128), visc_ref[lev], F32)] * 2
        rate = [jnp.full((8, 128), rate_ref[lev], F32)] * 2
        amp = table_ref[seed, lev]

        def coefs(step, r, c):
            if r < 2:
                s = speeds_ref[step, 0, lev, :, cols_at(c)].astype(F32)[8 * r : 8 * r + 8]
                t = speeds_ref[step, 1, lev, :, cols_at(c)].astype(F32)[8 * r : 8 * r + 8]
                return s, t, upwind_ref[step, lev, rows_at(r), cols_at(c)]
            s, t, m = (halo_coef(lev, kind, step, c) for kind in range(3))
            return s, t, m.astype(I32)

        def edges(step, count):
            to_first = lax.rem(253 - 8 * lev, 128)
            to_last = lax.rem(251 - 8 * lev, 128)
            out = []
            for ref in (edge_state, edge_delta):
                out.append([pltpu.roll(ref[step, 0, rows_at(r), :], to_first, 1) for r in range(count)])
                out.append([pltpu.roll(ref[step, 1, rows_at(r), :], to_last, 1) for r in range(count)])
            return out

        state = [[state_ref[lev, rows_at(r), cols_at(c)] for c in range(2)] for r in range(2)]
        state.append([halo_state(p, odd, c) for c in range(2)])
        delta = [[delta_ref[0, lev, rows_at(r), cols_at(c)] * amp for c in range(2)] for r in range(2)]
        delta.append([halo_delta(lev, c) * amp for c in range(2)])
        state, delta = run(state, delta, visc, rate, coefs, edges, lambda *unused: None)
        for r in range(2):
            for c in range(2):
                finals[lev, rows_at(r), cols_at(c)] = state[r][c]
                delta_out[0, lev, rows_at(r), cols_at(c)] = delta[r][c]

    def body(p, carry):
        one_level(p, 0)
        one_level(p, 1)
        return carry

    lax.fori_loop(0, LEV // 2, body, 0)
    state_out[...] = finals[pl.ds(first, 2)]


def call(kernel, shapes, specs, scratch=(), cost=None):
    out = [jax.ShapeDtypeStruct(shape, F32) for shape in shapes]
    single = len(out) == 1
    return pl.pallas_call(
        kernel,
        out_shape=out[0] if single else out,
        in_specs=specs,
        out_specs=VMEM if single else [VMEM] * len(out),
        scratch_shapes=scratch,
        compiler_params=pltpu.CompilerParams(vmem_limit_bytes=12 * 2**20),
        cost_estimate=pl.CostEstimate(flops=cost or 100000, bytes_accessed=cost or 100000, transcendentals=0),
    )


def per_device(perturbation, seed_ids, amp_table, start_state, speeds, upwind, viscosity, reaction):
    n_lat, n_lon, n_ens = lax.axis_size("lat"), lax.axis_size("lon"), lax.axis_size("ens")
    north = [(i, i + 1) for i in range(n_lat - 1)]
    south = [(j, i) for i, j in north]
    eastward = [(i, (i + 1) % n_lon) for i in range(n_lon)]
    westward = [(j, i) for i, j in eastward]

    def run(kernel, shapes, specs, *args):
        return call(kernel, shapes, specs)(*args)

    other = lax.ppermute(start_state, "ens", [(i, i ^ 1) for i in range(n_ens)])
    columns = run(pack_columns, [(NCD, 16, 128)], [VMEM] * 3, perturbation, speeds, upwind)
    from_west = lax.ppermute(columns, "lon", eastward)
    from_east = lax.ppermute(columns, "lon", westward)
    quad = run(join_pair, [(4, 16, 256)], [VMEM] * 2, start_state, other)
    ahead = [lax.ppermute(quad, "ens", [((i + 2 * j) % n_ens, i) for i in range(n_ens)]) for j in (1, 2, 3)]
    strips, down, up = run(
        pack_rows, [(NCD, 16, 256), (LEV + 1, 24, 256), (LEV + 1, 24, 256)], [VMEM] * 6,
        perturbation, speeds, upwind, columns, from_west, from_east,
    )
    cd_north = lax.ppermute(down, "lat", south)
    cd_south = lax.ppermute(up, "lat", north)
    states, state_columns = run(join_all, [(LEV, 16, 256), (1, 16, 128)], [VMEM] * 4, quad, *ahead)
    state_west = lax.ppermute(state_columns, "lon", eastward)
    state_east = lax.ppermute(state_columns, "lon", westward)
    state_strip, state_down, state_up = run(
        state_rows, [(16, 256), (9, 8, 256), (9, 8, 256)], [VMEM] * 4,
        states, state_columns, state_west, state_east,
    )
    st_north = lax.ppermute(state_down, "lat", south)
    st_south = lax.ppermute(state_up, "lat", north)
    edge = pltpu.VMEM((STEPS, 2, 24, 128), F32)
    return call(
        advance,
        [(1, LEV, 16, 256), (2, 16, 256)],
        [SMEM] * 4 + [VMEM] * 10,
        scratch=[edge, edge, pltpu.VMEM((LEV, 16, 256), F32)],
        cost=10000000,
    )(
        seed_ids, amp_table, viscosity, reaction,
        perturbation, speeds, upwind, strips, cd_north, cd_south,
        states, state_strip, st_north, st_south,
    )


def solution(mesh):
    step = jax.shard_map(
        per_device,
        mesh=mesh,
        in_specs=(
            P("ens", None, "lat", "lon"),
            P("ens"),
            P(),
            P("ens", "lat", "lon"),
            P(None, None, None, "lat", "lon"),
            P(None, None, "lat", "lon"),
            P(),
            P(),
        ),
        out_specs=(P("ens", None, "lat", "lon"), P("ens", "lat", "lon")),
        check_vma=False,
    )
    return lambda *args: tuple(step(*args))
```

```python
import jax
import jax.numpy as jnp
from jax import lax
from jax.experimental import pallas as pl
from jax.experimental.pallas import tpu as pltpu
from jax.sharding import PartitionSpec as P


F32 = jnp.float32
I32 = jnp.int32
STEPS = 4
LEV = 16
COEF = 3
NCD = 1 + 3 * COEF
VMEM = pl.BlockSpec(memory_space=pltpu.VMEM)
SMEM = pl.BlockSpec(memory_space=pltpu.SMEM)
HBM = pl.BlockSpec(memory_space=pltpu.HBM)
LIMIT = 8 * 2**20


def lanes():
    return lax.broadcasted_iota(I32, (8, 128), 1)


def subs():
    return lax.broadcasted_iota(I32, (8, 128), 0)


def rows_at(r):
    return pl.ds(8 * r, 8)


def cols_at(c):
    return pl.ds(128 * c, 128)


def is_odd(axis):
    return jnp.full((8, 128), lax.rem(lax.axis_index(axis), 2), I32) == 1


def own_tiles(delta_ref, speeds_ref, upwind_ref, a, lev, c):
    if a == 0:
        return [delta_ref[0, lev, rows_at(r), cols_at(c)] for r in range(2)]
    step, kind = divmod(a - 1, 3)
    if kind < 2:
        both = speeds_ref[step, kind, lev, :, cols_at(c)].astype(F32)
        return [both[0:8], both[8:16]]
    return [upwind_ref[step, lev, rows_at(r), cols_at(c)].astype(F32) for r in range(2)]


def slot(acc, left, right, lev):
    lane = lanes()
    edge = pltpu.roll(jnp.where(lane < 64, left, right), 8 * lev + 4, 1)
    return jnp.where(lane // 8 == lev, edge, acc)


def pack_columns(
    seed_hbm, table_hbm, visc_hbm, rate_hbm, state_hbm, delta_hbm, speeds_hbm, upwind_hbm,
    out_ref, state_ref, delta_ref, speeds_ref, upwind_ref, const_ref,
    seed_ref, table_ref, visc_ref, rate_ref, small_sems, sems, last_sems,
):
    small = [
        pltpu.make_async_copy(src, dst, small_sems.at[n])
        for n, (src, dst) in enumerate(
            ((seed_hbm, seed_ref), (table_hbm, table_ref), (visc_hbm, visc_ref), (rate_hbm, rate_ref))
        )
    ]
    groups = [[pltpu.make_async_copy(delta_hbm, delta_ref, sems.at[0])]]
    last = [pltpu.make_async_copy(state_hbm, state_ref, last_sems.at[0])]
    for step in range(STEPS):
        pair = []
        for n, (src, dst) in enumerate(((speeds_hbm, speeds_ref), (upwind_hbm, upwind_ref))):
            sem = sems.at[1 + 2 * step + n] if step < COEF else last_sems.at[1 + n]
            pair.append(pltpu.make_async_copy(src.at[step], dst.at[step], sem))
        if step < COEF:
            groups.append(pair)
        else:
            last += pair
    for copy in small + [c for group in groups for c in group] + last:
        copy.start()
    for copy in small:
        copy.wait()
    lane = lanes()
    seed = seed_ref[0]
    spread = [jnp.zeros((8, 128), F32)] * 3
    for lev in range(LEV):
        here = (visc_ref[lev], rate_ref[lev], table_ref[seed, lev])
        for q in range(3):
            tile = jnp.full((8, 128), here[q], F32)
            const_ref[lev, q] = tile
            spread[q] = jnp.where(lane // 8 == lev, tile, spread[q])
    for q in range(3):
        const_ref[LEV, q] = spread[q]
    for a in range(NCD):
        if a % 3 < 2 and (a == 0 or a % 3 == 1):
            for copy in groups[(a + 2) // 3]:
                copy.wait()
        acc = [jnp.zeros((8, 128), F32)] * 2
        for lev in range(LEV):
            left = own_tiles(delta_ref, speeds_ref, upwind_ref, a, lev, 0)
            right = own_tiles(delta_ref, speeds_ref, upwind_ref, a, lev, 1)
            acc = [slot(acc[r], left[r], right[r], lev) for r in range(2)]
        for r in range(2):
            out_ref[a, rows_at(r), :] = acc[r]
    for copy in last:
        copy.wait()


def strip_tile(own_ref, inner_ref, outer_ref, a, r, c):
    half, odd = lanes() % 8 < 4, is_odd("lon")
    own = own_ref[a, rows_at(r), :]
    inner, outer = inner_ref[a, rows_at(r), :], outer_ref[a, rows_at(r), :]
    if c == 0:
        return jnp.where(half, jnp.where(odd, inner, outer), own)
    return jnp.where(half, own, jnp.where(odd, outer, inner))


def join_pair(own_ref, other_ref, out_ref):
    half = lax.rem(lax.axis_index("ens"), 2)
    out_ref[pl.ds(2 * half, 2)] = own_ref[...]
    out_ref[pl.ds(2 - 2 * half, 2)] = other_ref[...]


def merge_rows(pieces):
    sub = subs()
    acc = jnp.zeros((8, 128), F32)
    for tile, shift, first, last in pieces:
        if shift % 8:
            tile = pltpu.roll(tile, shift % 8, 0)
        acc = jnp.where((sub >= first) & (sub <= last), tile, acc)
    return acc


def pack_rows(delta_ref, speeds_ref, upwind_ref, own_ref, near_ref, far_ref, strip_ref, inner_ref, outer_ref):
    odd = is_odd("lat")

    def put(lev, c, tiles):
        for kind in range(3):
            k0, k1, k2 = (tiles[1 + 3 * step + kind] for step in range(3))
            d = tiles[0]
            low = [(k0[0], 0, 0, 2), (k1[0], 3, 3, 4), (k2[0], 5, 5, 5)]
            high = [(k0[1], 0, 5, 7), (k1[1], -3, 3, 4), (k2[1], -5, 2, 2)]
            if kind == 0:
                low.append((d[0], 6, 6, 7))
                high.append((d[1], -4, 0, 1))
            if kind == 1:
                low.append((d[0], 4, 6, 7))
                high.append((d[1], -6, 0, 1))
            down, up = merge_rows(low), merge_rows(high)
            inner_ref[lev, rows_at(kind), cols_at(c)] = jnp.where(odd, down, up)
            outer_ref[lev, rows_at(kind), cols_at(c)] = jnp.where(odd, up, down)

    for c in range(2):
        tiles = []
        for a in range(NCD):
            pair = [strip_tile(own_ref, near_ref, far_ref, a, r, c) for r in range(2)]
            for r in range(2):
                strip_ref[a, rows_at(r), cols_at(c)] = pair[r]
            tiles.append(pair)
        put(LEV, c, tiles)

    def body(lev, carry):
        for c in range(2):
            put(lev, c, [own_tiles(delta_ref, speeds_ref, upwind_ref, a, lev, c) for a in range(NCD)])
        return carry

    lax.fori_loop(0, LEV, body, 0)


def join_all(b0_ref, b1_ref, b2_ref, b3_ref, out_ref, columns_ref):
    mine = lax.axis_index("ens") // 2
    acc = [jnp.zeros((8, 128), F32)] * 2
    for ahead, ref in enumerate((b0_ref, b1_ref, b2_ref, b3_ref)):
        base = 4 * (mine ^ ahead)
        out_ref[pl.ds(base, 4)] = ref[...]
        for i in range(4):
            for r in range(2):
                left, right = (ref[i, rows_at(r), cols_at(c)] for c in range(2))
                acc[r] = slot(acc[r], left, right, base + i)
    for r in range(2):
        columns_ref[0, rows_at(r), :] = acc[r]


def state_rows(state_ref, own_ref, near_ref, far_ref, strip_ref, inner_ref, outer_ref):
    low, odd = subs() < 4, is_odd("lat")
    for c in range(2):
        pair = [strip_tile(own_ref, near_ref, far_ref, 0, r, c) for r in range(2)]
        for r in range(2):
            strip_ref[rows_at(r), cols_at(c)] = pair[r]
        inner_ref[8, :, cols_at(c)] = jnp.where(odd, pair[0], pair[1])
        outer_ref[8, :, cols_at(c)] = jnp.where(odd, pair[1], pair[0])
        for p in range(8):
            a0, a1 = (state_ref[2 * p, rows_at(r), cols_at(c)] for r in range(2))
            b0, b1 = (pltpu.roll(state_ref[2 * p + 1, rows_at(r), cols_at(c)], 4, 0) for r in range(2))
            down, up = jnp.where(low, a0, b0), jnp.where(low, b1, a1)
            inner_ref[p, :, cols_at(c)] = jnp.where(odd, down, up)
            outer_ref[p, :, cols_at(c)] = jnp.where(odd, up, down)


def weights(s, t, m, v):
    vs, vt = v + s, v + t
    eastward, northward = (m & 1) == 1, m >= 2
    return (
        ((1.0 - 2.0 * v) - vs) - vt,
        jnp.where(eastward, vs, v),
        jnp.where(eastward, v, vs),
        jnp.where(northward, vt, v),
        jnp.where(northward, v, vt),
    )


def own_weights(speeds_ref, upwind_ref, strip_ref, const_ref, out_ref):
    def put(lev, step, r, c, tiles):
        for q, tile in enumerate(tiles):
            out_ref[lev, ((step * 2 + r) * 2 + c) * 5 + q] = tile

    for step in range(COEF):
        for r in range(2):
            for c in range(2):
                s, t, m = (strip_ref[1 + 3 * step + kind, rows_at(r), cols_at(c)] for kind in range(3))
                put(LEV, step, r, c, weights(s, t, m.astype(I32), const_ref[LEV, 0]))

    def body(lev, carry):
        v = const_ref[lev, 0]
        for step in range(STEPS):
            for c in range(2):
                s = speeds_ref[step, 0, lev, :, cols_at(c)].astype(F32)
                t = speeds_ref[step, 1, lev, :, cols_at(c)].astype(F32)
                for r in range(2):
                    m = upwind_ref[step, lev, rows_at(r), cols_at(c)]
                    put(lev, step, r, c, weights(s[8 * r : 8 * r + 8], t[8 * r : 8 * r + 8], m, v))
        return carry

    lax.fori_loop(0, LEV, body, 0)


def halo_weights(inner_ref, outer_ref, const_ref, out_ref, delta_ref):
    sub, odd = subs(), is_odd("lat")
    band = lax.axis_index("lat")
    inside = jnp.where(
        sub < 4,
        jnp.where(band < lax.axis_size("lat") - 1, 1.0, 0.0).astype(F32),
        jnp.where(band > 0, 1.0, 0.0).astype(F32),
    )
    keep = [(sub <= 2, sub >= 5), (sub <= 1, sub >= 6), (sub <= 0, sub >= 7)]

    def body(lev, carry):
        v, amp = const_ref[lev, 0] * inside, const_ref[lev, 2]
        for c in range(2):
            inner = [inner_ref[lev, rows_at(kind), cols_at(c)] for kind in range(3)]
            outer = [outer_ref[lev, rows_at(kind), cols_at(c)] for kind in range(3)]
            north = [jnp.where(odd, outer[kind], inner[kind]) for kind in range(3)]
            south = [jnp.where(odd, inner[kind], outer[kind]) for kind in range(3)]
            for step, shift in enumerate((0, 3, 5)):
                low, high = keep[step]
                stm = []
                for kind in range(3):
                    n, s = north[kind], south[kind]
                    if shift:
                        n, s = pltpu.roll(n, 8 - shift, 0), pltpu.roll(s, shift, 0)
                    stm.append(jnp.where(low, n, jnp.where(high, s, 0.0)))
                for q, tile in enumerate(weights(stm[0], stm[1], stm[2].astype(I32), v)):
                    out_ref[lev, (step * 2 + c) * 5 + q] = tile
            n0, n1 = pltpu.roll(north[0], 2, 0), pltpu.roll(north[1], 4, 0)
            s0, s1 = pltpu.roll(south[0], 4, 0), pltpu.roll(south[1], 6, 0)
            tile = jnp.where(sub < 2, n0, jnp.where(sub < 4, n1, jnp.where(sub < 6, s0, s1)))
            delta_ref[lev, :, cols_at(c)] = tile * amp
        return carry

    lax.fori_loop(0, LEV + 1, body, 0)


def advance(
    const_ref, delta_ref, strip_ref, own_ref, halo_ref, delta_halo_ref,
    state_ref, state_strip_ref, inner_ref, outer_ref,
    delta_out, state_out,
    edge_state, edge_delta, finals, work,
):
    lane = lanes()
    first = 2 * lax.axis_index("ens")
    outer_first = (subs() // 4 == 0) == is_odd("lat")

    def halo_state(p, odd, c):
        inner, outer = inner_ref[p, :, cols_at(c)], outer_ref[p, :, cols_at(c)]
        if odd:
            return pltpu.roll(jnp.where(outer_first, inner, outer), 4, 0)
        return jnp.where(outer_first, outer, inner)

    def sides(f, fix_west, fix_east):
        west, east = [], []
        for r, (left, right) in enumerate(f):
            wl, wr = pltpu.roll(left, 1, 1), pltpu.roll(right, 1, 1)
            el, er = pltpu.roll(left, 127, 1), pltpu.roll(right, 127, 1)
            if fix_west is None:
                west.append((wl, wr))
                east.append((el, er))
            else:
                west.append((jnp.where(lane == 0, fix_west[r], wl), jnp.where(lane == 0, wl, wr)))
                east.append((jnp.where(lane == 127, er, el), jnp.where(lane == 127, fix_east[r], er)))
        return west, east

    def ends(f, buf, count):
        for c in range(2):
            for r in range(3):
                buf[c, pl.ds(8 + 8 * r, 8), :] = f[r][c]
            buf[c, pl.ds(0, 8), :] = f[2][c]
            if count == 3:
                buf[c, pl.ds(32, 8), :] = f[0][c]
        below = [[buf[c, pl.ds(8 * r + 7, 8), :] for c in range(2)] for r in range(count)]
        above = [[buf[c, pl.ds(8 * r + 9, 8), :] for c in range(2)] for r in range(count)]
        return below, above

    def run(lev, odd, state, delta, edges, before):
        rate = const_ref[lev, 1]
        for step in range(STEPS):
            before(step, state, delta)
            if step == STEPS - 1 and edges is None:
                return state, delta
            count = 3 if step < STEPS - 1 else 2
            fixes = [None] * 4 if edges is None else edges(step, count)
            ws, es = sides(state[:count], fixes[0], fixes[1])
            wd, ed = sides(delta[:count], fixes[2], fixes[3])
            ss, ns = ends(state, work.at[odd, step % 2, 0], count)
            sd, nd = ends(delta, work.at[odd, step % 2, 1], count)
            next_state, next_delta = [], []
            for r in range(count):
                row_s, row_d = [], []
                for c in range(2):
                    if r < 2:
                        at = [own_ref[lev, ((step * 2 + r) * 2 + c) * 5 + q] for q in range(5)]
                    else:
                        at = [halo_ref[lev, (step * 2 + c) * 5 + q] for q in range(5)]
                    c0, cw, ce, cs, cn = at
                    f, d = state[r][c], delta[r][c]
                    loss = rate * (f * f)
                    row_s.append(
                        ((c0 - loss) * f + cw * ws[r][c]) + (ce * es[r][c] + cs * ss[r][c]) + cn * ns[r][c]
                    )
                    row_d.append(
                        ((c0 - 3.0 * loss) * d + cw * wd[r][c]) + (ce * ed[r][c] + cs * sd[r][c]) + cn * nd[r][c]
                    )
                next_state.append(row_s)
                next_delta.append(row_d)
            state, delta = next_state, next_delta
        return state, delta

    def strip_before(step, state, delta):
        for r in range(3):
            for c in range(2):
                edge_state[step, c, rows_at(r), :] = state[r][c]
                edge_delta[step, c, rows_at(r), :] = delta[r][c]

    amp = const_ref[LEV, 2]
    state = [[state_strip_ref[rows_at(r), cols_at(c)] for c in range(2)] for r in range(2)]
    state.append([halo_state(8, 0, c) for c in range(2)])
    delta = [[strip_ref[0, rows_at(r), cols_at(c)] * amp for c in range(2)] for r in range(2)]
    delta.append([delta_halo_ref[LEV, :, cols_at(c)] for c in range(2)])
    run(LEV, 0, state, delta, None, strip_before)

    def one_level(p, odd):
        lev = 2 * p + odd
        amp = const_ref[lev, 2]

        def edges(step, count):
            to_first = lax.rem(253 - 8 * lev, 128)
            to_last = lax.rem(251 - 8 * lev, 128)
            out = []
            for ref in (edge_state, edge_delta):
                out.append([pltpu.roll(ref[step, 0, rows_at(r), :], to_first, 1) for r in range(count)])
                out.append([pltpu.roll(ref[step, 1, rows_at(r), :], to_last, 1) for r in range(count)])
            return out

        state = [[state_ref[lev, rows_at(r), cols_at(c)] for c in range(2)] for r in range(2)]
        state.append([halo_state(p, odd, c) for c in range(2)])
        delta = [[delta_ref[0, lev, rows_at(r), cols_at(c)] * amp for c in range(2)] for r in range(2)]
        delta.append([delta_halo_ref[lev, :, cols_at(c)] for c in range(2)])
        state, delta = run(lev, odd, state, delta, edges, lambda *unused: None)
        for r in range(2):
            for c in range(2):
                finals[lev, rows_at(r), cols_at(c)] = state[r][c]
                delta_out[0, lev, rows_at(r), cols_at(c)] = delta[r][c]

    def body(p, carry):
        one_level(p, 0)
        one_level(p, 1)
        return carry

    lax.fori_loop(0, LEV // 2, body, 0)
    state_out[...] = finals[pl.ds(first, 2)]


def call(kernel, shapes, specs, scratch=(), cost=100000):
    out = [jax.ShapeDtypeStruct(shape, dtype) for shape, dtype in ((*e, F32)[:2] for e in shapes)]
    single = len(out) == 1
    return pl.pallas_call(
        kernel,
        out_shape=out[0] if single else out,
        in_specs=specs,
        out_specs=VMEM if single else [VMEM] * len(out),
        scratch_shapes=scratch,
        compiler_params=pltpu.CompilerParams(vmem_limit_bytes=LIMIT),
        cost_estimate=pl.CostEstimate(flops=cost, bytes_accessed=cost, transcendentals=0),
    )


def per_device(perturbation, seed_ids, amp_table, start_state, speeds, upwind, viscosity, reaction):
    n_lat, n_lon, n_ens = lax.axis_size("lat"), lax.axis_size("lon"), lax.axis_size("ens")
    lat_inner = [(i, i ^ 1) for i in range(n_lat)]
    lat_outer = [(i, ((i + 1) ^ 1) - 1) for i in range(1, n_lat - 1)]
    lon_inner = [(i, i ^ 1) for i in range(n_lon)]
    lon_outer = [(i, (((i + 1) ^ 1) - 1) % n_lon) for i in range(n_lon)]

    def run(kernel, shapes, specs, *args, **more):
        return call(kernel, [(shape,) if isinstance(shape[0], int) else shape for shape in shapes], specs, **more)(*args)

    other = lax.ppermute(start_state, "ens", [(i, i ^ 1) for i in range(n_ens)])
    columns, state, delta, fast, wind, consts = run(
        pack_columns,
        [
            (NCD, 16, 128), start_state.shape, perturbation.shape, (speeds.shape, speeds.dtype), (upwind.shape, upwind.dtype),
            (LEV + 1, 3, 8, 128),
        ],
        [HBM] * 8,
        seed_ids,
        *(
            pltpu.with_memory_space_constraint(x, pltpu.HBM)
            for x in (amp_table, viscosity, reaction, start_state, perturbation, speeds, upwind)
        ),
        scratch=[
            pltpu.SMEM(seed_ids.shape, I32), pltpu.SMEM(amp_table.shape, F32),
            pltpu.SMEM(viscosity.shape, F32), pltpu.SMEM(reaction.shape, F32),
            pltpu.SemaphoreType.DMA((4,)), pltpu.SemaphoreType.DMA((1 + 2 * COEF,)),
            pltpu.SemaphoreType.DMA((3,)),
        ],
    )
    near = lax.ppermute(columns, "lon", lon_inner)
    far = lax.ppermute(columns, "lon", lon_outer)
    quad = run(join_pair, [(4, 16, 256)], [VMEM] * 2, state, other)
    ahead = [lax.ppermute(quad, "ens", [(i, i ^ (2 * j)) for i in range(n_ens)]) for j in (1, 2, 3)]
    strips, down, up = run(
        pack_rows, [(NCD, 16, 256), (LEV + 1, 24, 256), (LEV + 1, 24, 256)], [VMEM] * 6,
        delta, fast, wind, columns, near, far,
    )
    cd_north = lax.ppermute(down, "lat", lat_inner)
    cd_south = lax.ppermute(up, "lat", lat_outer)
    states, state_columns = run(join_all, [(LEV, 16, 256), (1, 16, 128)], [VMEM] * 4, quad, *ahead)
    state_west = lax.ppermute(state_columns, "lon", lon_inner)
    state_east = lax.ppermute(state_columns, "lon", lon_outer)
    own = run(own_weights, [(LEV + 1, 20 * STEPS, 8, 128)], [VMEM] * 4, fast, wind, strips, consts)
    state_strip, state_down, state_up = run(
        state_rows, [(16, 256), (9, 8, 256), (9, 8, 256)], [VMEM] * 4,
        states, state_columns, state_west, state_east,
    )
    st_north = lax.ppermute(state_down, "lat", lat_inner)
    st_south = lax.ppermute(state_up, "lat", lat_outer)
    halo, delta_halo = run(
        halo_weights, [(LEV + 1, 10 * COEF, 8, 128), (LEV + 1, 8, 256)], [VMEM] * 3,
        cd_north, cd_south, consts,
    )
    edge = pltpu.VMEM((STEPS, 2, 24, 128), F32)
    return run(
        advance, [(1, LEV, 16, 256), (2, 16, 256)], [VMEM] * 10,
        consts, delta, strips, own, halo, delta_halo, states, state_strip, st_north, st_south,
        scratch=[edge, edge, pltpu.VMEM((LEV, 16, 256), F32), pltpu.VMEM((2, 2, 2, 2, 40, 128), F32)],
        cost=10000000,
    )


def solution(mesh):
    step = jax.shard_map(
        per_device,
        mesh=mesh,
        in_specs=(
            P("ens", None, "lat", "lon"),
            P("ens"),
            P(),
            P("ens", "lat", "lon"),
            P(None, None, None, "lat", "lon"),
            P(None, None, "lat", "lon"),
            P(),
            P(),
        ),
        out_specs=(P("ens", None, "lat", "lon"), P("ens", "lat", "lon")),
        check_vma=False,
    )
    return lambda *args: tuple(step(*args))
```

```python
import itertools

import jax
import jax.numpy as jnp
from jax import lax
from jax.experimental import pallas as pl
from jax.experimental.pallas import tpu as pltpu
from jax.sharding import PartitionSpec as P


F32 = jnp.float32
I32 = jnp.int32
STEPS = 4
LEV = 16
COEF = 3
NCD = 1 + 3 * COEF
VMEM = pl.BlockSpec(memory_space=pltpu.VMEM)
SMEM = pl.BlockSpec(memory_space=pltpu.SMEM)
HBM = pl.BlockSpec(memory_space=pltpu.HBM)
LIMIT = 8 * 2**20
GROUP = 2


def lanes():
    return lax.broadcasted_iota(I32, (8, 128), 1)


def subs():
    return lax.broadcasted_iota(I32, (8, 128), 0)


def rows_at(r):
    return pl.ds(8 * r, 8)


def cols_at(c):
    return pl.ds(128 * c, 128)


def is_odd(axis):
    return jnp.full((8, 128), lax.rem(lax.axis_index(axis), 2), I32) == 1


def own_tiles(delta_ref, speeds_ref, upwind_ref, a, lev, c):
    if a == 0:
        return [delta_ref[0, lev, rows_at(r), cols_at(c)] for r in range(2)]
    step, kind = divmod(a - 1, 3)
    if kind < 2:
        both = speeds_ref[step, kind, lev, :, cols_at(c)].astype(F32)
        return [both[0:8], both[8:16]]
    return [upwind_ref[step, lev, rows_at(r), cols_at(c)].astype(F32) for r in range(2)]


def slot(acc, left, right, lev):
    lane = lanes()
    edge = pltpu.roll(jnp.where(lane < 64, left, right), 8 * lev + 4, 1)
    return jnp.where(lane // 8 == lev, edge, acc)


def pack_columns(
    visc_hbm, rate_hbm, state_hbm, delta_hbm, speeds_hbm, upwind_hbm,
    out_ref, state_ref, delta_ref, speeds_ref, upwind_ref, const_ref,
    visc_ref, rate_ref, small_sems, sems, last_sems,
):
    small = [
        pltpu.make_async_copy(src, dst, small_sems.at[n])
        for n, (src, dst) in enumerate(((visc_hbm, visc_ref), (rate_hbm, rate_ref)))
    ]
    groups = [[pltpu.make_async_copy(delta_hbm, delta_ref, sems.at[0])]]
    last = [pltpu.make_async_copy(state_hbm, state_ref, last_sems.at[0])]
    for step in range(COEF):
        groups.append([])
        for n, (src, dst) in enumerate(((speeds_hbm, speeds_ref), (upwind_hbm, upwind_ref))):
            groups[-1].append(pltpu.make_async_copy(src.at[step], dst.at[step], sems.at[1 + 2 * step + n]))
    for copy in small + [c for group in groups for c in group] + last:
        copy.start()
    for copy in small:
        copy.wait()
    lane = lanes()
    spread = [jnp.zeros((8, 128), F32)] * 2
    for lev in range(LEV):
        here = (visc_ref[lev], rate_ref[lev])
        for q in range(2):
            tile = jnp.full((8, 128), here[q], F32)
            const_ref[lev, q] = tile
            spread[q] = jnp.where(lane // 8 == lev, tile, spread[q])
    for q in range(2):
        const_ref[LEV, q] = spread[q]
    for a in range(NCD):
        if a % 3 < 2 and (a == 0 or a % 3 == 1):
            for copy in groups[(a + 2) // 3]:
                copy.wait()
        acc = [jnp.zeros((8, 128), F32)] * 2
        for lev in range(LEV):
            left = own_tiles(delta_ref, speeds_ref, upwind_ref, a, lev, 0)
            right = own_tiles(delta_ref, speeds_ref, upwind_ref, a, lev, 1)
            acc = [slot(acc[r], left[r], right[r], lev) for r in range(2)]
        for r in range(2):
            out_ref[a, rows_at(r), :] = acc[r]
    for copy in last:
        copy.wait()


def strip_tile(own_ref, inner_ref, outer_ref, a, r, c):
    half, odd = lanes() % 8 < 4, is_odd("lon")
    own = own_ref[a, rows_at(r), :]
    inner, outer = inner_ref[a, rows_at(r), :], outer_ref[a, rows_at(r), :]
    if c == 0:
        return jnp.where(half, jnp.where(odd, inner, outer), own)
    return jnp.where(half, own, jnp.where(odd, outer, inner))


def join_pair(own_ref, other_ref, out_ref):
    half = lax.rem(lax.axis_index("ens"), 2)
    out_ref[pl.ds(2 * half, 2)] = own_ref[...]
    out_ref[pl.ds(2 - 2 * half, 2)] = other_ref[...]


def merge_rows(pieces):
    sub = subs()
    acc = jnp.zeros((8, 128), F32)
    for tile, shift, first, last in pieces:
        if shift % 8:
            tile = pltpu.roll(tile, shift % 8, 0)
        acc = jnp.where((sub >= first) & (sub <= last), tile, acc)
    return acc


def pack_rows(delta_ref, speeds_ref, upwind_ref, own_ref, near_ref, far_ref, strip_ref, inner_ref, outer_ref):
    odd = is_odd("lat")

    def put(lev, c, tiles):
        for kind in range(3):
            k0, k1, k2 = (tiles[1 + 3 * step + kind] for step in range(3))
            d = tiles[0]
            low = [(k0[0], 0, 0, 2), (k1[0], 3, 3, 4), (k2[0], 5, 5, 5)]
            high = [(k0[1], 0, 5, 7), (k1[1], -3, 3, 4), (k2[1], -5, 2, 2)]
            if kind == 0:
                low.append((d[0], 6, 6, 7))
                high.append((d[1], -4, 0, 1))
            if kind == 1:
                low.append((d[0], 4, 6, 7))
                high.append((d[1], -6, 0, 1))
            down, up = merge_rows(low), merge_rows(high)
            inner_ref[lev, rows_at(kind), cols_at(c)] = jnp.where(odd, down, up)
            outer_ref[lev, rows_at(kind), cols_at(c)] = jnp.where(odd, up, down)

    for c in range(2):
        tiles = []
        for a in range(NCD):
            pair = [strip_tile(own_ref, near_ref, far_ref, a, r, c) for r in range(2)]
            for r in range(2):
                strip_ref[a, rows_at(r), cols_at(c)] = pair[r]
            tiles.append(pair)
        put(LEV, c, tiles)

    def body(lev, carry):
        for c in range(2):
            put(lev, c, [own_tiles(delta_ref, speeds_ref, upwind_ref, a, lev, c) for a in range(NCD)])
        return carry

    lax.fori_loop(0, LEV, body, 0)


def join_all(b0_ref, b1_ref, b2_ref, b3_ref, out_ref, columns_ref):
    mine = lax.axis_index("ens") // 2
    acc = [jnp.zeros((8, 128), F32)] * 2
    for ahead, ref in enumerate((b0_ref, b1_ref, b2_ref, b3_ref)):
        base = 4 * (mine ^ ahead)
        out_ref[pl.ds(base, 4)] = ref[...]
        for i in range(4):
            for r in range(2):
                left, right = (ref[i, rows_at(r), cols_at(c)] for c in range(2))
                acc[r] = slot(acc[r], left, right, base + i)
    for r in range(2):
        columns_ref[0, rows_at(r), :] = acc[r]


def state_rows(state_ref, own_ref, near_ref, far_ref, strip_ref, inner_ref, outer_ref):
    low, odd = subs() < 4, is_odd("lat")
    for c in range(2):
        pair = [strip_tile(own_ref, near_ref, far_ref, 0, r, c) for r in range(2)]
        for r in range(2):
            strip_ref[rows_at(r), cols_at(c)] = pair[r]
        inner_ref[8, :, cols_at(c)] = jnp.where(odd, pair[0], pair[1])
        outer_ref[8, :, cols_at(c)] = jnp.where(odd, pair[1], pair[0])
        for p in range(8):
            a0, a1 = (state_ref[2 * p, rows_at(r), cols_at(c)] for r in range(2))
            b0, b1 = (pltpu.roll(state_ref[2 * p + 1, rows_at(r), cols_at(c)], 4, 0) for r in range(2))
            down, up = jnp.where(low, a0, b0), jnp.where(low, b1, a1)
            inner_ref[p, :, cols_at(c)] = jnp.where(odd, down, up)
            outer_ref[p, :, cols_at(c)] = jnp.where(odd, up, down)


def weights(s, t, m, v):
    vs, vt = v + s, v + t
    eastward, northward = (m & 1) == 1, m >= 2
    return (
        ((1.0 - 2.0 * v) - vs) - vt,
        jnp.where(eastward, vs, v),
        jnp.where(eastward, v, vs),
        jnp.where(northward, vt, v),
        jnp.where(northward, v, vt),
    )


def own_weights(
    speeds_hbm, upwind_hbm, early_speeds, early_upwind, strip_ref, const_ref, out_ref, late_speeds, late_upwind, sems
):
    copies = [
        pltpu.make_async_copy(speeds_hbm.at[COEF], late_speeds, sems.at[0]),
        pltpu.make_async_copy(upwind_hbm.at[COEF], late_upwind, sems.at[1]),
    ]
    for copy in copies:
        copy.start()

    def put(lev, step, r, c, tiles):
        for q, tile in enumerate(tiles):
            out_ref[lev, ((step * 2 + r) * 2 + c) * 5 + q] = tile

    for step in range(COEF):
        for r in range(2):
            for c in range(2):
                s, t, m = (strip_ref[1 + 3 * step + kind, rows_at(r), cols_at(c)] for kind in range(3))
                put(LEV, step, r, c, weights(s, t, m.astype(I32), const_ref[LEV, 0]))

    def level(lev, steps):
        v = const_ref[lev, 0]
        for step in steps:
            speeds_ref, upwind_ref = late_speeds, late_upwind
            if step < COEF:
                speeds_ref, upwind_ref = early_speeds.at[step], early_upwind.at[step]
            for c in range(2):
                s = speeds_ref[0, lev, :, cols_at(c)].astype(F32)
                t = speeds_ref[1, lev, :, cols_at(c)].astype(F32)
                for r in range(2):
                    m = upwind_ref[lev, rows_at(r), cols_at(c)]
                    put(lev, step, r, c, weights(s[8 * r : 8 * r + 8], t[8 * r : 8 * r + 8], m, v))

    def early(lev, carry):
        level(lev, range(COEF))
        return carry

    def late(lev, carry):
        level(lev, (COEF,))
        return carry

    lax.fori_loop(0, LEV, early, 0)
    for copy in copies:
        copy.wait()
    lax.fori_loop(0, LEV, late, 0)


def halo_weights(
    seed_ref, table_hbm, inner_ref, outer_ref, const_ref, out_ref, delta_ref, amp_ref, table_ref, sem
):
    copy = pltpu.make_async_copy(table_hbm, table_ref, sem)
    copy.start()
    lane = lanes()
    sub, odd = subs(), is_odd("lat")
    band = lax.axis_index("lat")
    inside = jnp.where(
        sub < 4,
        jnp.where(band < lax.axis_size("lat") - 1, 1.0, 0.0).astype(F32),
        jnp.where(band > 0, 1.0, 0.0).astype(F32),
    )
    keep = [(sub <= 2, sub >= 5), (sub <= 1, sub >= 6), (sub <= 0, sub >= 7)]

    def body(lev, carry):
        v = const_ref[lev, 0] * inside
        for c in range(2):
            inner = [inner_ref[lev, rows_at(kind), cols_at(c)] for kind in range(3)]
            outer = [outer_ref[lev, rows_at(kind), cols_at(c)] for kind in range(3)]
            north = [jnp.where(odd, outer[kind], inner[kind]) for kind in range(3)]
            south = [jnp.where(odd, inner[kind], outer[kind]) for kind in range(3)]
            for step, shift in enumerate((0, 3, 5)):
                low, high = keep[step]
                stm = []
                for kind in range(3):
                    n, s = north[kind], south[kind]
                    if shift:
                        n, s = pltpu.roll(n, 8 - shift, 0), pltpu.roll(s, shift, 0)
                    stm.append(jnp.where(low, n, jnp.where(high, s, 0.0)))
                for q, tile in enumerate(weights(stm[0], stm[1], stm[2].astype(I32), v)):
                    out_ref[lev, (step * 2 + c) * 5 + q] = tile
            n0, n1 = pltpu.roll(north[0], 2, 0), pltpu.roll(north[1], 4, 0)
            s0, s1 = pltpu.roll(south[0], 4, 0), pltpu.roll(south[1], 6, 0)
            tile = jnp.where(sub < 2, n0, jnp.where(sub < 4, n1, jnp.where(sub < 6, s0, s1)))
            delta_ref[lev, :, cols_at(c)] = tile
        return carry

    lax.fori_loop(0, LEV + 1, body, 0)
    copy.wait()
    seed = seed_ref[0]
    spread = jnp.zeros((8, 128), F32)
    for lev in range(LEV):
        tile = jnp.full((8, 128), table_ref[seed, lev], F32)
        amp_ref[lev] = tile
        spread = jnp.where(lane // 8 == lev, tile, spread)
    amp_ref[LEV] = spread


def advance(
    const_ref, amp_ref, delta_ref, strip_ref, own_ref, halo_ref, delta_halo_ref,
    state_ref, state_strip_ref, inner_ref, outer_ref,
    delta_out, state_out,
    edge_state, edge_delta, finals, work,
):
    lane = lanes()
    first = 2 * lax.axis_index("ens")
    outer_first = (subs() // 4 == 0) == is_odd("lat")

    def halo_state(p, odd, c):
        inner, outer = inner_ref[p, :, cols_at(c)], outer_ref[p, :, cols_at(c)]
        if odd:
            return pltpu.roll(jnp.where(outer_first, inner, outer), 4, 0)
        return jnp.where(outer_first, outer, inner)

    def sides(f, fix):
        west, east = [], []
        for r, (left, right) in enumerate(f):
            wl, wr = pltpu.roll(left, 1, 1), pltpu.roll(right, 1, 1)
            el, er = pltpu.roll(left, 127, 1), pltpu.roll(right, 127, 1)
            if fix is None:
                west.append((wl, wr))
                east.append((el, er))
            else:
                west.append((jnp.where(lane == 0, fix[r], wl), jnp.where(lane == 0, wl, wr)))
                east.append((jnp.where(lane == 127, er, el), jnp.where(lane == 127, fix[r], er)))
        return west, east

    def ends(f, buf, count):
        for c in range(2):
            for r in range(3):
                buf[c, pl.ds(8 + 8 * r, 8), :] = f[r][c]
            buf[c, pl.ds(0, 8), :] = f[2][c]
            if count == 3:
                buf[c, pl.ds(32, 8), :] = f[0][c]
        below = [[buf[c, pl.ds(8 * r + 7, 8), :] for c in range(2)] for r in range(count)]
        above = [[buf[c, pl.ds(8 * r + 9, 8), :] for c in range(2)] for r in range(count)]
        return below, above

    def run(lev, place, state, delta, edges):
        rate = const_ref[lev, 1]
        for step in range(STEPS):
            yield
            count = 3 if step < STEPS - 1 else 2
            fixes = (None, None) if edges is None else edges(step, count)
            ws, es = sides(state[:count], fixes[0])
            wd, ed = sides(delta[:count], fixes[1])
            if edges is None:
                for ref, west, east in ((edge_state, ws, es), (edge_delta, wd, ed)):
                    for r in range(count):
                        ref[step, rows_at(r), :] = jnp.where(lane % 8 == 4, west[r][0], east[r][1])
                if step == STEPS - 1:
                    return
            ss, ns = ends(state, work.at[place, step % 2, 0], count)
            sd, nd = ends(delta, work.at[place, step % 2, 1], count)
            next_state, next_delta = [], []
            for r in range(count):
                row_s, row_d = [], []
                for c in range(2):
                    if r < 2:
                        at = [own_ref[lev, ((step * 2 + r) * 2 + c) * 5 + q] for q in range(5)]
                    else:
                        at = [halo_ref[lev, (step * 2 + c) * 5 + q] for q in range(5)]
                    c0, cw, ce, cs, cn = at
                    f, d = state[r][c], delta[r][c]
                    loss = rate * (f * f)
                    row_s.append(
                        ((c0 - loss) * f + cw * ws[r][c]) + (ce * es[r][c] + cs * ss[r][c]) + cn * ns[r][c]
                    )
                    row_d.append(
                        ((c0 - 3.0 * loss) * d + cw * wd[r][c]) + (ce * ed[r][c] + cs * sd[r][c]) + cn * nd[r][c]
                    )
                next_state.append(row_s)
                next_delta.append(row_d)
            state, delta = next_state, next_delta
        for r in range(2):
            for c in range(2):
                finals[lev, rows_at(r), cols_at(c)] = state[r][c]
                delta_out[0, lev, rows_at(r), cols_at(c)] = delta[r][c]

    amp = amp_ref[LEV]
    state = [[state_strip_ref[rows_at(r), cols_at(c)] for c in range(2)] for r in range(2)]
    state.append([halo_state(8, 0, c) for c in range(2)])
    delta = [[strip_ref[0, rows_at(r), cols_at(c)] * amp for c in range(2)] for r in range(2)]
    delta.append([delta_halo_ref[LEV, :, cols_at(c)] * amp for c in range(2)])
    for _ in run(LEV, 0, state, delta, None):
        pass

    def one_level(p, place):
        odd = place % 2
        p = GROUP // 2 * p + place // 2
        lev = 2 * p + odd
        amp = amp_ref[lev]

        def edges(step, count):
            return [
                [pltpu.roll(ref[step, rows_at(r), :], 124 - 8 * lev, 1) for r in range(count)]
                for ref in (edge_state, edge_delta)
            ]

        state = [[state_ref[lev, rows_at(r), cols_at(c)] for c in range(2)] for r in range(2)]
        state.append([halo_state(p, odd, c) for c in range(2)])
        delta = [[delta_ref[0, lev, rows_at(r), cols_at(c)] * amp for c in range(2)] for r in range(2)]
        delta.append([delta_halo_ref[lev, :, cols_at(c)] * amp for c in range(2)])
        return run(lev, place, state, delta, edges)

    def body(p, carry):
        for _ in itertools.zip_longest(*(one_level(p, place) for place in range(GROUP))):
            pass
        return carry

    lax.fori_loop(0, LEV // GROUP, body, 0)
    state_out[...] = finals[pl.ds(first, 2)]


def call(kernel, shapes, specs, scratch=(), cost=100000):
    out = [jax.ShapeDtypeStruct(shape, dtype) for shape, dtype in ((*e, F32)[:2] for e in shapes)]
    single = len(out) == 1
    return pl.pallas_call(
        kernel,
        out_shape=out[0] if single else out,
        in_specs=specs,
        out_specs=VMEM if single else [VMEM] * len(out),
        scratch_shapes=scratch,
        compiler_params=pltpu.CompilerParams(vmem_limit_bytes=LIMIT),
        cost_estimate=pl.CostEstimate(flops=cost, bytes_accessed=cost, transcendentals=0),
    )


def per_device(perturbation, seed_ids, amp_table, start_state, speeds, upwind, viscosity, reaction):
    n_lat, n_lon, n_ens = lax.axis_size("lat"), lax.axis_size("lon"), lax.axis_size("ens")
    lat_inner = [(i, i ^ 1) for i in range(n_lat)]
    lat_outer = [(i, ((i + 1) ^ 1) - 1) for i in range(1, n_lat - 1)]
    lon_inner = [(i, i ^ 1) for i in range(n_lon)]
    lon_outer = [(i, (((i + 1) ^ 1) - 1) % n_lon) for i in range(n_lon)]

    def run(kernel, shapes, specs, *args, **more):
        return call(kernel, [(shape,) if isinstance(shape[0], int) else shape for shape in shapes], specs, **more)(*args)

    other = lax.ppermute(start_state, "ens", [(i, i ^ 1) for i in range(n_ens)])
    columns, state, delta, fast, wind, consts = run(
        pack_columns,
        [
            (NCD, 16, 128), start_state.shape, perturbation.shape, ((COEF, *speeds.shape[1:]), speeds.dtype), ((COEF, *upwind.shape[1:]), upwind.dtype),
            (LEV + 1, 2, 8, 128),
        ],
        [HBM] * 6,
        *(
            pltpu.with_memory_space_constraint(x, pltpu.HBM)
            for x in (viscosity, reaction, start_state, perturbation, speeds, upwind)
        ),
        scratch=[
            pltpu.SMEM(viscosity.shape, F32), pltpu.SMEM(reaction.shape, F32),
            pltpu.SemaphoreType.DMA((2,)), pltpu.SemaphoreType.DMA((1 + 2 * COEF,)),
            pltpu.SemaphoreType.DMA((1,)),
        ],
    )
    near = lax.ppermute(columns, "lon", lon_inner)
    far = lax.ppermute(columns, "lon", lon_outer)
    quad = run(join_pair, [(4, 16, 256)], [VMEM] * 2, state, other)
    ahead = [lax.ppermute(quad, "ens", [(i, i ^ (2 * j)) for i in range(n_ens)]) for j in (1, 2, 3)]
    strips, down, up = run(
        pack_rows, [(NCD, 16, 256), (LEV + 1, 24, 256), (LEV + 1, 24, 256)], [VMEM] * 6,
        delta, fast, wind, columns, near, far,
    )
    cd_north = lax.ppermute(down, "lat", lat_inner)
    cd_south = lax.ppermute(up, "lat", lat_outer)
    states, state_columns = run(join_all, [(LEV, 16, 256), (1, 16, 128)], [VMEM] * 4, quad, *ahead)
    state_west = lax.ppermute(state_columns, "lon", lon_inner)
    state_east = lax.ppermute(state_columns, "lon", lon_outer)
    own = run(
        own_weights, [(LEV + 1, 20 * STEPS, 8, 128)], [HBM] * 2 + [VMEM] * 4,
        *(pltpu.with_memory_space_constraint(x, pltpu.HBM) for x in (speeds, upwind)), fast, wind, strips, consts,
        scratch=[
            pltpu.VMEM(speeds.shape[1:], speeds.dtype), pltpu.VMEM(upwind.shape[1:], upwind.dtype),
            pltpu.SemaphoreType.DMA((2,)),
        ],
    )
    state_strip, state_down, state_up = run(
        state_rows, [(16, 256), (9, 8, 256), (9, 8, 256)], [VMEM] * 4,
        states, state_columns, state_west, state_east,
    )
    st_north = lax.ppermute(state_down, "lat", lat_inner)
    st_south = lax.ppermute(state_up, "lat", lat_outer)
    halo, delta_halo, amp = run(
        halo_weights, [(LEV + 1, 10 * COEF, 8, 128), (LEV + 1, 8, 256), (LEV + 1, 8, 128)],
        [SMEM, HBM] + [VMEM] * 3,
        seed_ids, pltpu.with_memory_space_constraint(amp_table, pltpu.HBM), cd_north, cd_south, consts,
        scratch=[pltpu.SMEM(amp_table.shape, F32), pltpu.SemaphoreType.DMA],
    )
    edge = pltpu.VMEM((STEPS, 24, 128), F32)
    return run(
        advance, [(1, LEV, 16, 256), (2, 16, 256)], [VMEM] * 11,
        consts, amp, delta, strips, own, halo, delta_halo, states, state_strip, st_north, st_south,
        scratch=[edge, edge, pltpu.VMEM((LEV, 16, 256), F32), pltpu.VMEM((GROUP, 2, 2, 2, 40, 128), F32)],
        cost=10000000,
    )


def solution(mesh):
    step = jax.shard_map(
        per_device,
        mesh=mesh,
        in_specs=(
            P("ens", None, "lat", "lon"),
            P("ens"),
            P(),
            P("ens", "lat", "lon"),
            P(None, None, None, "lat", "lon"),
            P(None, None, "lat", "lon"),
            P(),
            P(),
        ),
        out_specs=(P("ens", None, "lat", "lon"), P("ens", "lat", "lon")),
        check_vma=False,
    )
    return lambda *args: tuple(step(*args))
```

```python
import itertools

import jax
import jax.numpy as jnp
from jax import lax
from jax.experimental import pallas as pl
from jax.experimental.pallas import tpu as pltpu
from jax.sharding import PartitionSpec as P


F32 = jnp.float32
I32 = jnp.int32
STEPS = 4
LEV = 16
COEF = 3
NCD = 1 + 3 * COEF
VMEM = pl.BlockSpec(memory_space=pltpu.VMEM)
SMEM = pl.BlockSpec(memory_space=pltpu.SMEM)
HBM = pl.BlockSpec(memory_space=pltpu.HBM)
LIMIT = 8 * 2**20
GROUP = 8


def lanes():
    return lax.broadcasted_iota(I32, (8, 128), 1)


def subs():
    return lax.broadcasted_iota(I32, (8, 128), 0)


def rows_at(r):
    return pl.ds(8 * r, 8)


def cols_at(c):
    return pl.ds(128 * c, 128)


def is_odd(axis):
    return jnp.full((8, 128), lax.rem(lax.axis_index(axis), 2), I32) == 1


def own_tiles(delta_ref, speeds_ref, upwind_ref, a, lev, c):
    if a == 0:
        return [delta_ref[0, lev, rows_at(r), cols_at(c)] for r in range(2)]
    step, kind = divmod(a - 1, 3)
    if kind < 2:
        both = speeds_ref[step, kind, lev, :, cols_at(c)].astype(F32)
        return [both[0:8], both[8:16]]
    return [upwind_ref[step, lev, rows_at(r), cols_at(c)].astype(F32) for r in range(2)]


def slot(acc, left, right, lev):
    lane = lanes()
    edge = pltpu.roll(jnp.where(lane < 64, left, right), 8 * lev + 4, 1)
    return jnp.where(lane // 8 == lev, edge, acc)


def pack_columns(
    visc_hbm, rate_hbm, state_hbm, delta_hbm, speeds_hbm, upwind_hbm,
    out_ref, state_ref, delta_ref, speeds_ref, upwind_ref, const_ref,
    visc_ref, rate_ref, small_sems, sems, last_sems,
):
    small = [
        pltpu.make_async_copy(src, dst, small_sems.at[n])
        for n, (src, dst) in enumerate(((visc_hbm, visc_ref), (rate_hbm, rate_ref)))
    ]
    groups = [[pltpu.make_async_copy(delta_hbm, delta_ref, sems.at[0])]]
    last = [pltpu.make_async_copy(state_hbm, state_ref, last_sems.at[0])]
    for step in range(COEF):
        groups.append([])
        for n, (src, dst) in enumerate(((speeds_hbm, speeds_ref), (upwind_hbm, upwind_ref))):
            groups[-1].append(pltpu.make_async_copy(src.at[step], dst.at[step], sems.at[1 + 2 * step + n]))
    for copy in small + [c for group in groups for c in group] + last:
        copy.start()
    for copy in small:
        copy.wait()
    lane = lanes()
    spread = [jnp.zeros((8, 128), F32)] * 2
    for lev in range(LEV):
        here = (visc_ref[lev], rate_ref[lev])
        for q in range(2):
            tile = jnp.full((8, 128), here[q], F32)
            const_ref[lev, q] = tile
            spread[q] = jnp.where(lane // 8 == lev, tile, spread[q])
    for q in range(2):
        const_ref[LEV, q] = spread[q]
    for a in range(NCD):
        if a % 3 < 2 and (a == 0 or a % 3 == 1):
            for copy in groups[(a + 2) // 3]:
                copy.wait()
        acc = [jnp.zeros((8, 128), F32)] * 2
        for lev in range(LEV):
            left = own_tiles(delta_ref, speeds_ref, upwind_ref, a, lev, 0)
            right = own_tiles(delta_ref, speeds_ref, upwind_ref, a, lev, 1)
            acc = [slot(acc[r], left[r], right[r], lev) for r in range(2)]
        for r in range(2):
            out_ref[a, rows_at(r), :] = acc[r]
    for copy in last:
        copy.wait()


def strip_tile(own_ref, inner_ref, outer_ref, a, r, c):
    half, odd = lanes() % 8 < 4, is_odd("lon")
    own = own_ref[a, rows_at(r), :]
    inner, outer = inner_ref[a, rows_at(r), :], outer_ref[a, rows_at(r), :]
    if c == 0:
        return jnp.where(half, jnp.where(odd, inner, outer), own)
    return jnp.where(half, own, jnp.where(odd, outer, inner))


def join_pair(own_ref, other_ref, out_ref):
    half = lax.rem(lax.axis_index("ens"), 2)
    out_ref[pl.ds(2 * half, 2)] = own_ref[...]
    out_ref[pl.ds(2 - 2 * half, 2)] = other_ref[...]


def merge_rows(pieces):
    sub = subs()
    acc = jnp.zeros((8, 128), F32)
    for tile, shift, first, last in pieces:
        if shift % 8:
            tile = pltpu.roll(tile, shift % 8, 0)
        acc = jnp.where((sub >= first) & (sub <= last), tile, acc)
    return acc


def pack_rows(delta_ref, speeds_ref, upwind_ref, own_ref, near_ref, far_ref, strip_ref, inner_ref, outer_ref):
    odd = is_odd("lat")

    def put(lev, c, tiles):
        for kind in range(3):
            k0, k1, k2 = (tiles[1 + 3 * step + kind] for step in range(3))
            d = tiles[0]
            low = [(k0[0], 0, 0, 2), (k1[0], 3, 3, 4), (k2[0], 5, 5, 5)]
            high = [(k0[1], 0, 5, 7), (k1[1], -3, 3, 4), (k2[1], -5, 2, 2)]
            if kind == 0:
                low.append((d[0], 6, 6, 7))
                high.append((d[1], -4, 0, 1))
            if kind == 1:
                low.append((d[0], 4, 6, 7))
                high.append((d[1], -6, 0, 1))
            down, up = merge_rows(low), merge_rows(high)
            inner_ref[lev, rows_at(kind), cols_at(c)] = jnp.where(odd, down, up)
            outer_ref[lev, rows_at(kind), cols_at(c)] = jnp.where(odd, up, down)

    for c in range(2):
        tiles = []
        for a in range(NCD):
            pair = [strip_tile(own_ref, near_ref, far_ref, a, r, c) for r in range(2)]
            for r in range(2):
                strip_ref[a, rows_at(r), cols_at(c)] = pair[r]
            tiles.append(pair)
        put(LEV, c, tiles)

    def body(lev, carry):
        for c in range(2):
            put(lev, c, [own_tiles(delta_ref, speeds_ref, upwind_ref, a, lev, c) for a in range(NCD)])
        return carry

    lax.fori_loop(0, LEV, body, 0)


def join_all(b0_ref, b1_ref, b2_ref, b3_ref, out_ref, columns_ref):
    mine = lax.axis_index("ens") // 2
    acc = [jnp.zeros((8, 128), F32)] * 2
    for ahead, ref in enumerate((b0_ref, b1_ref, b2_ref, b3_ref)):
        base = 4 * (mine ^ ahead)
        out_ref[pl.ds(base, 4)] = ref[...]
        for i in range(4):
            for r in range(2):
                left, right = (ref[i, rows_at(r), cols_at(c)] for c in range(2))
                acc[r] = slot(acc[r], left, right, base + i)
    for r in range(2):
        columns_ref[0, rows_at(r), :] = acc[r]


def state_rows(state_ref, own_ref, near_ref, far_ref, strip_ref, inner_ref, outer_ref):
    low, odd = subs() < 4, is_odd("lat")
    for c in range(2):
        pair = [strip_tile(own_ref, near_ref, far_ref, 0, r, c) for r in range(2)]
        for r in range(2):
            strip_ref[rows_at(r), cols_at(c)] = pair[r]
        inner_ref[8, :, cols_at(c)] = jnp.where(odd, pair[0], pair[1])
        outer_ref[8, :, cols_at(c)] = jnp.where(odd, pair[1], pair[0])
        for p in range(8):
            a0, a1 = (state_ref[2 * p, rows_at(r), cols_at(c)] for r in range(2))
            b0, b1 = (pltpu.roll(state_ref[2 * p + 1, rows_at(r), cols_at(c)], 4, 0) for r in range(2))
            down, up = jnp.where(low, a0, b0), jnp.where(low, b1, a1)
            inner_ref[p, :, cols_at(c)] = jnp.where(odd, down, up)
            outer_ref[p, :, cols_at(c)] = jnp.where(odd, up, down)


def weights(s, t, m, v):
    vs, vt = v + s, v + t
    eastward, northward = (m & 1) == 1, m >= 2
    return (
        ((1.0 - 2.0 * v) - vs) - vt,
        jnp.where(eastward, vs, v),
        jnp.where(eastward, v, vs),
        jnp.where(northward, vt, v),
        jnp.where(northward, v, vt),
    )


def own_weights(
    seed_ref, table_hbm, speeds_hbm, upwind_hbm, early_speeds, early_upwind, strip_ref, const_ref,
    out_ref, amp_ref, table_ref, late_speeds, late_upwind, sems,
):
    lane = lanes()
    copies = [
        pltpu.make_async_copy(table_hbm, table_ref, sems.at[2]),
        pltpu.make_async_copy(speeds_hbm.at[COEF], late_speeds, sems.at[0]),
        pltpu.make_async_copy(upwind_hbm.at[COEF], late_upwind, sems.at[1]),
    ]
    for copy in copies:
        copy.start()

    def put(lev, step, r, c, tiles):
        for q, tile in enumerate(tiles):
            out_ref[lev, ((step * 2 + r) * 2 + c) * 5 + q] = tile

    for step in range(COEF):
        for r in range(2):
            for c in range(2):
                s, t, m = (strip_ref[1 + 3 * step + kind, rows_at(r), cols_at(c)] for kind in range(3))
                put(LEV, step, r, c, weights(s, t, m.astype(I32), const_ref[LEV, 0]))

    def level(lev, steps):
        v = const_ref[lev, 0]
        for step in steps:
            speeds_ref, upwind_ref = late_speeds, late_upwind
            if step < COEF:
                speeds_ref, upwind_ref = early_speeds.at[step], early_upwind.at[step]
            for c in range(2):
                s = speeds_ref[0, lev, :, cols_at(c)].astype(F32)
                t = speeds_ref[1, lev, :, cols_at(c)].astype(F32)
                for r in range(2):
                    m = upwind_ref[lev, rows_at(r), cols_at(c)]
                    put(lev, step, r, c, weights(s[8 * r : 8 * r + 8], t[8 * r : 8 * r + 8], m, v))

    def early(lev, carry):
        level(lev, range(COEF))
        return carry

    def late(lev, carry):
        level(lev, (COEF,))
        return carry

    lax.fori_loop(0, LEV, early, 0)
    for copy in copies:
        copy.wait()
    lax.fori_loop(0, LEV, late, 0)
    seed = seed_ref[0]
    spread = jnp.zeros((8, 128), F32)
    for lev in range(LEV):
        tile = jnp.full((8, 128), table_ref[seed, lev], F32)
        amp_ref[lev] = tile
        spread = jnp.where(lane // 8 == lev, tile, spread)
    amp_ref[LEV] = spread


def halo_weights(inner_ref, outer_ref, const_ref, out_ref, delta_ref):
    sub, odd = subs(), is_odd("lat")
    band = lax.axis_index("lat")
    inside = jnp.where(
        sub < 4,
        jnp.where(band < lax.axis_size("lat") - 1, 1.0, 0.0).astype(F32),
        jnp.where(band > 0, 1.0, 0.0).astype(F32),
    )
    keep = [(sub <= 2, sub >= 5), (sub <= 1, sub >= 6), (sub <= 0, sub >= 7)]

    def body(lev, carry):
        v = const_ref[lev, 0] * inside
        for c in range(2):
            inner = [inner_ref[lev, rows_at(kind), cols_at(c)] for kind in range(3)]
            outer = [outer_ref[lev, rows_at(kind), cols_at(c)] for kind in range(3)]
            north = [jnp.where(odd, outer[kind], inner[kind]) for kind in range(3)]
            south = [jnp.where(odd, inner[kind], outer[kind]) for kind in range(3)]
            for step, shift in enumerate((0, 3, 5)):
                low, high = keep[step]
                stm = []
                for kind in range(3):
                    n, s = north[kind], south[kind]
                    if shift:
                        n, s = pltpu.roll(n, 8 - shift, 0), pltpu.roll(s, shift, 0)
                    stm.append(jnp.where(low, n, jnp.where(high, s, 0.0)))
                for q, tile in enumerate(weights(stm[0], stm[1], stm[2].astype(I32), v)):
                    out_ref[lev, (step * 2 + c) * 5 + q] = tile
            n0, n1 = pltpu.roll(north[0], 2, 0), pltpu.roll(north[1], 4, 0)
            s0, s1 = pltpu.roll(south[0], 4, 0), pltpu.roll(south[1], 6, 0)
            tile = jnp.where(sub < 2, n0, jnp.where(sub < 4, n1, jnp.where(sub < 6, s0, s1)))
            delta_ref[lev, :, cols_at(c)] = tile
        return carry

    lax.fori_loop(0, LEV + 1, body, 0)


def sides(f, fix):
    west, east, lane = [], [], lanes()
    for r, (left, right) in enumerate(f):
        wl, wr = pltpu.roll(left, 1, 1), pltpu.roll(right, 1, 1)
        el, er = pltpu.roll(left, 127, 1), pltpu.roll(right, 127, 1)
        if fix is None:
            west.append((wl, wr))
            east.append((el, er))
        else:
            west.append((jnp.where(lane == 0, fix[r], wl), jnp.where(lane == 0, wl, wr)))
            east.append((jnp.where(lane == 127, er, el), jnp.where(lane == 127, fix[r], er)))
    return west, east


def ends(f, buf, count):
    for c in range(2):
        for r in range(3):
            buf[c, pl.ds(8 + 8 * r, 8), :] = f[r][c]
        buf[c, pl.ds(0, 8), :] = f[2][c]
        if count == 3:
            buf[c, pl.ds(32, 8), :] = f[0][c]
    below = [[buf[c, pl.ds(8 * r + 7, 8), :] for c in range(2)] for r in range(count)]
    above = [[buf[c, pl.ds(8 * r + 9, 8), :] for c in range(2)] for r in range(count)]
    return below, above


def first_step(
    amp_ref, delta_ref, strip_ref, own_ref, halo_ref, delta_halo_ref, state_ref, state_strip_ref,
    delta_out, state_out, work,
):
    lane = lanes()

    def seam(tiles):
        left, right = tiles
        return jnp.where(lane % 8 == 4, pltpu.roll(left, 1, 1), pltpu.roll(right, 127, 1))

    amp = amp_ref[LEV]
    seam_d = [seam([strip_ref[0, rows_at(r), cols_at(c)] * amp for c in range(2)]) for r in range(2)]
    seam_d.append(seam([delta_halo_ref[LEV, :, cols_at(c)] * amp for c in range(2)]))
    seam_s = [seam([state_strip_ref[rows_at(r), cols_at(c)] for c in range(2)]) for r in range(2)]

    def level(lev, place):
        amp = amp_ref[lev]
        state = [[state_ref[lev, rows_at(r), cols_at(c)] for c in range(2)] for r in range(2)]
        delta = [[delta_ref[0, lev, rows_at(r), cols_at(c)] * amp for c in range(2)] for r in range(2)]
        delta.append([delta_halo_ref[lev, :, cols_at(c)] * amp for c in range(2)])
        shift = 124 - 8 * lev
        ws, es = sides(state, [pltpu.roll(seam_s[r], shift, 1) for r in range(2)])
        wd, ed = sides(delta, [pltpu.roll(seam_d[r], shift, 1) for r in range(3)])
        sd, nd = ends(delta, work.at[place], 3)
        for r in range(3):
            for c in range(2):
                if r < 2:
                    c0, cw, ce, cs, cn = (own_ref[lev, (r * 2 + c) * 5 + q] for q in range(5))
                    state_out[lev, r * 2 + c] = c0 * state[r][c] + cw * ws[r][c] + ce * es[r][c]
                else:
                    c0, cw, ce, cs, cn = (halo_ref[lev, c * 5 + q] for q in range(5))
                delta_out[lev, r * 2 + c] = (
                    (c0 * delta[r][c] + cw * wd[r][c]) + (ce * ed[r][c] + cs * sd[r][c]) + cn * nd[r][c]
                )

    def body(p, carry):
        for place in range(GROUP):
            level(GROUP * p + place, place)
        return carry

    lax.fori_loop(0, LEV // GROUP, body, 0)


def advance(
    const_ref, amp_ref, delta_ref, strip_ref, own_ref, halo_ref, delta_halo_ref, delta_lin_ref, state_lin_ref,
    state_ref, state_strip_ref, inner_ref, outer_ref,
    delta_out, state_out,
    edge_state, edge_delta, finals, work,
):
    lane = lanes()
    first = 2 * lax.axis_index("ens")
    outer_first = (subs() // 4 == 0) == is_odd("lat")

    def halo_state(p, odd, c):
        inner, outer = inner_ref[p, :, cols_at(c)], outer_ref[p, :, cols_at(c)]
        if odd:
            return pltpu.roll(jnp.where(outer_first, inner, outer), 4, 0)
        return jnp.where(outer_first, outer, inner)

    def run(lev, place, state, delta, edges):
        rate = const_ref[lev, 1]
        for step in range(STEPS):
            yield
            count = 3 if step < STEPS - 1 else 2
            if step == 0 and edges is not None:
                (west,), (east,) = sides([state[2]], edges(0, 2))
                ss, ns = ends(state, work.at[place, 0, 0], 3)
                next_state, next_delta = [], []
                for r in range(3):
                    row_s, row_d = [], []
                    for c in range(2):
                        f, d = state[r][c], delta[r][c]
                        loss = rate * (f * f)
                        if r < 2:
                            cs, cn = (own_ref[lev, (r * 2 + c) * 5 + q] for q in (3, 4))
                            side = state_lin_ref[lev, r * 2 + c] - loss * f
                        else:
                            c0, cw, ce, cs, cn = (halo_ref[lev, c * 5 + q] for q in range(5))
                            side = ((c0 - loss) * f + cw * west[c]) + ce * east[c]
                        row_s.append(side + (cs * ss[r][c] + cn * ns[r][c]))
                        row_d.append(delta_lin_ref[lev, r * 2 + c] - (3.0 * loss) * d)
                    next_state.append(row_s)
                    next_delta.append(row_d)
                state, delta = next_state, next_delta
                continue
            fixes = (None, None) if edges is None else edges(step, count)
            ws, es = sides(state[:count], fixes[0])
            wd, ed = sides(delta[:count], fixes[1])
            if edges is None:
                for ref, west, east in ((edge_state, ws, es), (edge_delta, wd, ed)):
                    for r in range(count):
                        ref[step, rows_at(r), :] = jnp.where(lane % 8 == 4, west[r][0], east[r][1])
                if step == STEPS - 1:
                    return
            ss, ns = ends(state, work.at[place, step % 2, 0], count)
            sd, nd = ends(delta, work.at[place, step % 2, 1], count)
            next_state, next_delta = [], []
            for r in range(count):
                row_s, row_d = [], []
                for c in range(2):
                    if r < 2:
                        at = [own_ref[lev, ((step * 2 + r) * 2 + c) * 5 + q] for q in range(5)]
                    else:
                        at = [halo_ref[lev, (step * 2 + c) * 5 + q] for q in range(5)]
                    c0, cw, ce, cs, cn = at
                    f, d = state[r][c], delta[r][c]
                    loss = rate * (f * f)
                    row_s.append(
                        ((c0 - loss) * f + cw * ws[r][c]) + (ce * es[r][c] + cs * ss[r][c]) + cn * ns[r][c]
                    )
                    row_d.append(
                        ((c0 - 3.0 * loss) * d + cw * wd[r][c]) + (ce * ed[r][c] + cs * sd[r][c]) + cn * nd[r][c]
                    )
                next_state.append(row_s)
                next_delta.append(row_d)
            state, delta = next_state, next_delta
        for r in range(2):
            for c in range(2):
                finals[lev, rows_at(r), cols_at(c)] = state[r][c]
                delta_out[0, lev, rows_at(r), cols_at(c)] = delta[r][c]

    amp = amp_ref[LEV]
    state = [[state_strip_ref[rows_at(r), cols_at(c)] for c in range(2)] for r in range(2)]
    state.append([halo_state(8, 0, c) for c in range(2)])
    delta = [[strip_ref[0, rows_at(r), cols_at(c)] * amp for c in range(2)] for r in range(2)]
    delta.append([delta_halo_ref[LEV, :, cols_at(c)] * amp for c in range(2)])
    for _ in run(LEV, 0, state, delta, None):
        pass

    def one_level(p, place):
        odd = place % 2
        p = GROUP // 2 * p + place // 2
        lev = 2 * p + odd
        amp = amp_ref[lev]

        def edges(step, count):
            if step == 0:
                return [pltpu.roll(edge_state[0, rows_at(2), :], 124 - 8 * lev, 1)]
            return [
                [pltpu.roll(ref[step, rows_at(r), :], 124 - 8 * lev, 1) for r in range(count)]
                for ref in (edge_state, edge_delta)
            ]

        state = [[state_ref[lev, rows_at(r), cols_at(c)] for c in range(2)] for r in range(2)]
        state.append([halo_state(p, odd, c) for c in range(2)])
        delta = [[delta_ref[0, lev, rows_at(r), cols_at(c)] * amp for c in range(2)] for r in range(2)]
        delta.append([delta_halo_ref[lev, :, cols_at(c)] * amp for c in range(2)])
        return run(lev, place, state, delta, edges)

    def body(p, carry):
        for _ in itertools.zip_longest(*(one_level(p, place) for place in range(GROUP))):
            pass
        return carry

    lax.fori_loop(0, LEV // GROUP, body, 0)
    state_out[...] = finals[pl.ds(first, 2)]


def call(kernel, shapes, specs, scratch=(), cost=100000):
    out = [jax.ShapeDtypeStruct(shape, dtype) for shape, dtype in ((*e, F32)[:2] for e in shapes)]
    single = len(out) == 1
    return pl.pallas_call(
        kernel,
        out_shape=out[0] if single else out,
        in_specs=specs,
        out_specs=VMEM if single else [VMEM] * len(out),
        scratch_shapes=scratch,
        compiler_params=pltpu.CompilerParams(vmem_limit_bytes=LIMIT),
        cost_estimate=pl.CostEstimate(flops=cost, bytes_accessed=cost, transcendentals=0),
    )


def per_device(perturbation, seed_ids, amp_table, start_state, speeds, upwind, viscosity, reaction):
    n_lat, n_lon, n_ens = lax.axis_size("lat"), lax.axis_size("lon"), lax.axis_size("ens")
    lat_inner = [(i, i ^ 1) for i in range(n_lat)]
    lat_outer = [(i, ((i + 1) ^ 1) - 1) for i in range(1, n_lat - 1)]
    lon_inner = [(i, i ^ 1) for i in range(n_lon)]
    lon_outer = [(i, (((i + 1) ^ 1) - 1) % n_lon) for i in range(n_lon)]

    def run(kernel, shapes, specs, *args, **more):
        return call(kernel, [(shape,) if isinstance(shape[0], int) else shape for shape in shapes], specs, **more)(*args)

    other = lax.ppermute(start_state, "ens", [(i, i ^ 1) for i in range(n_ens)])
    columns, state, delta, fast, wind, consts = run(
        pack_columns,
        [
            (NCD, 16, 128), start_state.shape, perturbation.shape, ((COEF, *speeds.shape[1:]), speeds.dtype), ((COEF, *upwind.shape[1:]), upwind.dtype),
            (LEV + 1, 2, 8, 128),
        ],
        [HBM] * 6,
        *(
            pltpu.with_memory_space_constraint(x, pltpu.HBM)
            for x in (viscosity, reaction, start_state, perturbation, speeds, upwind)
        ),
        scratch=[
            pltpu.SMEM(viscosity.shape, F32), pltpu.SMEM(reaction.shape, F32),
            pltpu.SemaphoreType.DMA((2,)), pltpu.SemaphoreType.DMA((1 + 2 * COEF,)),
            pltpu.SemaphoreType.DMA((1,)),
        ],
    )
    near = lax.ppermute(columns, "lon", lon_inner)
    far = lax.ppermute(columns, "lon", lon_outer)
    quad = run(join_pair, [(4, 16, 256)], [VMEM] * 2, state, other)
    ahead = [lax.ppermute(quad, "ens", [(i, i ^ (2 * j)) for i in range(n_ens)]) for j in (1, 2, 3)]
    strips, down, up = run(
        pack_rows, [(NCD, 16, 256), (LEV + 1, 24, 256), (LEV + 1, 24, 256)], [VMEM] * 6,
        delta, fast, wind, columns, near, far,
    )
    cd_north = lax.ppermute(down, "lat", lat_inner)
    cd_south = lax.ppermute(up, "lat", lat_outer)
    states, state_columns = run(join_all, [(LEV, 16, 256), (1, 16, 128)], [VMEM] * 4, quad, *ahead)
    state_west = lax.ppermute(state_columns, "lon", lon_inner)
    state_east = lax.ppermute(state_columns, "lon", lon_outer)
    own, amp = run(
        own_weights, [(LEV + 1, 20 * STEPS, 8, 128), (LEV + 1, 8, 128)], [SMEM] + [HBM] * 3 + [VMEM] * 4,
        seed_ids, *(pltpu.with_memory_space_constraint(x, pltpu.HBM) for x in (amp_table, speeds, upwind)),
        fast, wind, strips, consts,
        scratch=[
            pltpu.SMEM(amp_table.shape, F32),
            pltpu.VMEM(speeds.shape[1:], speeds.dtype), pltpu.VMEM(upwind.shape[1:], upwind.dtype),
            pltpu.SemaphoreType.DMA((3,)),
        ],
    )
    state_strip, state_down, state_up = run(
        state_rows, [(16, 256), (9, 8, 256), (9, 8, 256)], [VMEM] * 4,
        states, state_columns, state_west, state_east,
    )
    st_north = lax.ppermute(state_down, "lat", lat_inner)
    st_south = lax.ppermute(state_up, "lat", lat_outer)
    halo, delta_halo = run(
        halo_weights, [(LEV + 1, 10 * COEF, 8, 128), (LEV + 1, 8, 256)], [VMEM] * 3,
        cd_north, cd_south, consts,
    )
    delta_lin, state_lin = run(
        first_step, [(LEV, 6, 8, 128), (LEV, 4, 8, 128)], [VMEM] * 8,
        amp, delta, strips, own, halo, delta_halo, states, state_strip,
        scratch=[pltpu.VMEM((GROUP, 2, 40, 128), F32)],
    )
    edge = pltpu.VMEM((STEPS, 24, 128), F32)
    return run(
        advance, [(1, LEV, 16, 256), (2, 16, 256)], [VMEM] * 13,
        consts, amp, delta, strips, own, halo, delta_halo, delta_lin, state_lin, states, state_strip, st_north, st_south,
        scratch=[edge, edge, pltpu.VMEM((LEV, 16, 256), F32), pltpu.VMEM((GROUP, 2, 2, 2, 40, 128), F32)],
        cost=10000000,
    )


def solution(mesh):
    step = jax.shard_map(
        per_device,
        mesh=mesh,
        in_specs=(
            P("ens", None, "lat", "lon"),
            P("ens"),
            P(),
            P("ens", "lat", "lon"),
            P(None, None, None, "lat", "lon"),
            P(None, None, "lat", "lon"),
            P(),
            P(),
        ),
        out_specs=(P("ens", None, "lat", "lon"), P("ens", "lat", "lon")),
        check_vma=False,
    )
    return lambda *args: tuple(step(*args))
```
